256 devices in a mesh: grid: 32 (over z, x_hi, core), orb: 8 (over y, x_lo).
Axes of the slice: x: 4 (x_hi: 2, x_lo: 2; x = x_hi * 2 + x_lo), y: 4, z: 8, core: 2. Of those that a mesh axis runs over, the one named last changes fastest.
Arguments:
- wave: float32 [2, 8, 128, 128, 128], P(None, 'orb', 'grid'), may hold values from -6 to 6
- potential: float32 [128, 128, 128], P('grid'), may hold values from -24 to 24
- occupations: float32 [8], P('orb'), may hold values from 0.01 to 0.1
- centres: int32 [3, 128], replicated, may hold values from 0 to 127, as said below
- species: int32 [128], replicated, may hold values from 0 to 1
- projectors: float32 [2, 16, 8, 256], replicated, may hold values from -0.75 to 0.75
- coupling: float32 [2, 8, 8], replicated, may hold values from -6 to 6
Outputs:
- update: float32 [2, 8, 128, 128, 128], P(None, 'orb', 'grid')
- density: float32 [128, 128, 128], P('grid', 'orb')
The draws below stay inside these ranges and needn't reach their ends.
Inputs may be any that keep to these rules, and one draw needn't show every extreme that they name: `centres`: each column is a grid point of the cell.
All inputs are finite; a program needn't handle non-finite values.
Results may differ from the reference program's by a relative error of at most 0.0003.
Values sent between devices are 32-bit elements; how exact they have to be, the bound alone decides.
No kernel may reach another device: no remote copies, remote signals or barrier semaphores. Data moves between devices by JAX's collectives and lax.ppermute only.
A program may use at most 64 MiB of HBM per device.

```python
import math
import jax
import jax.numpy as jnp
from jax import lax

SIDE = 128
NPROJ = 8
SPECIES = 2
BOX = 16
ATOMS = 128
ORBS = 8


def draw_centres(key, part):
    place_key = jax.random.fold_in(key, 11)
    pick_key = jax.random.fold_in(key, 12)
    coords = jax.random.randint(place_key, (3, ATOMS), 0, SIDE, dtype=jnp.int32)
    chosen = jax.random.randint(pick_key, (), 0, ATOMS, dtype=jnp.int32)
    second_atom = (chosen + 1) % ATOMS
    coords = coords.at[:, chosen].set(SIDE - 1)
    coords = coords.at[:, second_atom].set(0)
    return coords


def touch_ends(values, rng, smallest, top_value):
    spot = [jax.random.randint(jax.random.fold_in(rng, axis), (), 0, length) for axis, length in enumerate(values.shape)]
    longest = values.shape.index(max(values.shape))
    beside = spot[:longest] + [(spot[longest] + 1) % values.shape[longest]] + spot[longest + 1:]
    return values.at[tuple(spot)].set(smallest).at[tuple(beside)].set(top_value)


def levels(key, shape, split, smallest, largest):
    def one(position, parts):
        steps = jax.random.uniform(jax.random.fold_in(jax.random.fold_in(key, 6), position), (parts,), jnp.float32, smallest / len(split), largest / len(split))
        return jnp.repeat(jnp.exp(steps), shape[position] // parts).reshape((-1,) + (1,) * (len(shape) - position - 1))

    factor_of = one(*split[0])
    for cut in split[1:]:
        factor_of = factor_of * one(*cut)
    return factor_of


def noise(key, shape, deviation, bound, cuts=(), kind=jnp.bfloat16):
    entries = jax.random.normal(key, shape, jnp.float32) * deviation
    if len(cuts) > 0:
        entries = levels(key, shape, cuts, -0.22, 0.18) * entries
    return jnp.clip(entries, min=-bound, max=bound).astype(kind)


def setup_inputs(seed: int = 0) -> dict:
    key_of = jax.random.split(jax.random.key(seed), 8)
    return {
        "wave": noise(key_of[0], (2, ORBS, SIDE, SIDE, SIDE), 1.0, 6.0, ((1, 8), (2, 32)), jnp.float32),
        "potential": noise(key_of[1], (SIDE, SIDE, SIDE), 4.0, 24.0, ((0, 32),), jnp.float32),
        "occupations": jnp.clip(jnp.exp(math.log(0.1) - 2.3025851 * jax.random.uniform(key_of[2], (ORBS,), jnp.float32) ** levels(key_of[2], (ORBS,), ((0, 8),), -0.2, 0.2)), 0.01, 0.1),
        "centres": draw_centres(jax.random.fold_in(key_of[7], 71), 0),
        "species": touch_ends(jax.random.randint(key_of[4], (ATOMS,), 0, SPECIES), jax.random.fold_in(key_of[4], 1), 0, SPECIES - 1).astype(jnp.int32),
        "projectors": noise(key_of[5], (SPECIES, BOX, NPROJ, BOX * BOX), 0.125, 0.75, (), jnp.float32),
        "coupling": noise(key_of[6], (SPECIES, NPROJ, NPROJ), 1.0, 6.0, (), jnp.float32),
    }


spacing = 0.32
time_step = 0.1
highest = lax.Precision.HIGHEST


def frequencies(extent):
    counts = jnp.arange(extent, dtype=jnp.int32)
    signed = jnp.where(counts < extent // 2, counts, counts - extent)
    return signed.astype(jnp.float32) * (2.0 * math.pi / (extent * spacing))


def reference(wave, potential, occupations, centres, species, projectors, coupling):
    waves_k = frequencies(SIDE)
    kinetic = 0.5 * (waves_k[:, None, None] ** 2 + waves_k[None, :, None] ** 2 + waves_k[None, None, :] ** 2)

    def local_terms(halves):
        real_part, imag_part = halves
        spectrum = jnp.fft.fftn(lax.complex(real_part, imag_part))
        returned = jnp.fft.ifftn(spectrum * kinetic)
        return (jnp.real(returned) + potential * real_part, jnp.imag(returned) + potential * imag_part)

    h_real, h_imag = lax.map(local_terms, (wave[0], wave[1]))
    offsets = jnp.arange(BOX, dtype=jnp.int32) - BOX // 2
    flat_real = wave[0].reshape(ORBS, -1)
    flat_imag = wave[1].reshape(ORBS, -1)

    def add_atom(totals, atom_data):
        acc_real, acc_imag = totals
        centre, species_id = atom_data
        rows_x = (centre[0] + offsets) % SIDE
        rows_y = (centre[1] + offsets) % SIDE
        rows_z = (centre[2] + offsets) % SIDE
        grid_points = ((rows_x[:, None, None] * SIDE + rows_y[None, :, None]) * SIDE + rows_z[None, None, :]).reshape(-1).astype(jnp.int32)
        projector_rows = jnp.transpose(projectors[species_id], (1, 0, 2)).reshape(NPROJ, -1)
        coef_real = jnp.dot(projector_rows, flat_real[:, grid_points].T, precision=highest)
        coef_imag = jnp.dot(projector_rows, flat_imag[:, grid_points].T, precision=highest)
        scaled_real = jnp.dot(coupling[species_id], coef_real, precision=highest)
        scaled_imag = jnp.dot(coupling[species_id], coef_imag, precision=highest)
        acc_real = acc_real.at[:, grid_points].add(jnp.dot(scaled_real.T, projector_rows, precision=highest))
        acc_imag = acc_imag.at[:, grid_points].add(jnp.dot(scaled_imag.T, projector_rows, precision=highest))
        return (acc_real, acc_imag), None

    start_totals = (jnp.zeros(flat_real.shape, jnp.float32), jnp.zeros(flat_imag.shape, jnp.float32))
    (nl_real, nl_imag), _ = lax.scan(add_atom, start_totals, (centres.T, species))
    total_real = h_real + nl_real.reshape(h_real.shape)
    total_imag = h_imag + nl_imag.reshape(h_imag.shape)
    half_step = 0.5 * time_step
    update = jnp.stack([half_step * total_imag, -half_step * total_real])
    density = jnp.tensordot(occupations, wave[0] * wave[0] + wave[1] * wave[1], axes=1, precision=highest)
    return update, density
```

```python
import functools
import math

import jax
import jax.numpy as jnp
import numpy as np
from jax import lax
from jax.experimental import pallas as pl
from jax.experimental.pallas import tpu as pltpu
from jax.sharding import PartitionSpec as P

spacing = 0.32
time_step = 0.1
highest = lax.Precision.HIGHEST

SIDE = 128
BOX = 16
NPROJ = 8
PLANES = 4
PAD = SIDE + BOX
F32 = jnp.float32
BF16 = jnp.bfloat16


def permuted(value, axis, target):
    count = lax.axis_size(axis)
    return lax.ppermute(value, axis, [(source, target(source) % count) for source in range(count)])


def kinetic_matrix(extent):
    counts = np.arange(extent)
    signed = np.where(counts < extent // 2, counts, counts - extent)
    waves = signed * (2.0 * math.pi / (extent * spacing))
    angles = (counts[:, None] * counts[None, :] % extent) * (2.0 * math.pi / extent)
    column = (np.cos(angles) * (0.5 * waves**2)[None, :]).sum(axis=1) / extent
    return column[(counts[:, None] - counts[None, :]) % extent]


def kinetic_halves(extent):
    matrix = kinetic_matrix(extent).astype(np.float32)
    high = matrix.astype(BF16)
    low = (matrix - high.astype(np.float32)).astype(BF16)
    return jnp.asarray(high), jnp.asarray(low)


def halves(value):
    high = value.astype(BF16)
    return high, (value - high.astype(F32)).astype(BF16)


def times_right(value, high, low):
    first, second = halves(value)
    out = jnp.dot(first, high, preferred_element_type=F32)
    out = out + jnp.dot(second, high, preferred_element_type=F32)
    return out + jnp.dot(first, low, preferred_element_type=F32)


def times_left(high, low, value):
    first, second = halves(value)
    out = jnp.dot(high, first, preferred_element_type=F32)
    out = out + jnp.dot(high, second, preferred_element_type=F32)
    return out + jnp.dot(low, first, preferred_element_type=F32)


def whole(memory=pltpu.VMEM):
    return pl.BlockSpec(memory_space=memory)


def call(kernel, out_shape, specs, scratch=(), name=None, flops=1000000, moved=1000000):
    return pl.pallas_call(
        kernel,
        out_shape=out_shape,
        in_specs=specs,
        out_specs=jax.tree.map(lambda _: whole(), out_shape),
        scratch_shapes=list(scratch),
        name=name,
        cost_estimate=pl.CostEstimate(flops=flops, bytes_accessed=moved, transcendentals=0),
    )


def shape(*dims):
    return jax.ShapeDtypeStruct(dims, F32)


def pack_kernel(wave_ref, out_ref):
    for part in range(2):
        for plane in range(PLANES):
            out_ref[part, :, plane] = wave_ref[part, plane]


def density_kernel(occupation_ref, wave_ref, out_ref):
    occupation = occupation_ref[0]
    for plane in range(PLANES):
        real_part = wave_ref[0, plane]
        imag_part = wave_ref[1, plane]
        term = occupation * (real_part * real_part + imag_part * imag_part)
        for share in range(8):
            high, middle, low = share // 4, share // 2 % 2, share % 2
            out_ref[middle, high, low, plane] = term[share * 16 : share * 16 + 16]


def swap_blocks(tile, lane, row):
    for bit in (1, 2, 4):
        row_set = (row & bit) != 0
        lane_set = ((lane >> 4) & bit) != 0
        up = pltpu.roll(pltpu.roll(tile, 8 - bit, 0), 16 * bit, 1)
        down = pltpu.roll(pltpu.roll(tile, bit, 0), SIDE - 16 * bit, 1)
        tile = jnp.where(row_set == lane_set, tile, jnp.where(lane_set, up, down))
    return tile


def atom_place(first_ref, centres_ref, atom):
    depth = (first_ref[0] - centres_ref[0, atom] + (BOX // 2 + SIDE)) & (SIDE - 1)
    start_y = (centres_ref[1, atom] + (SIDE - BOX // 2)) & (SIDE - 1)
    start_z = (centres_ref[2, atom] + (SIDE - BOX // 2)) & (SIDE - 1)
    touched = ((depth + (PLANES - 1)) & (SIDE - 1)) < BOX + PLANES - 1
    return depth, start_y, start_z, touched


def table_row(depth, plane, kind):
    slot = (depth + plane) & (SIDE - 1)
    return jnp.where(slot < BOX, kind * BOX + slot, 2 * BOX)


def project_kernel(first_ref, centres_ref, species_ref, wave_ref, projectors_ref, coef_ref, table_ref, padded, sums):
    lane = lax.broadcasted_iota(jnp.int32, (8, SIDE), 1)
    row = lax.broadcasted_iota(jnp.int32, (8, SIDE), 0)

    def fill(index, carry):
        for half in range(2):
            tile = projectors_ref[index, :, half * SIDE : (half + 1) * SIDE]
            table_ref[index, half * 8 : half * 8 + 8, :] = swap_blocks(tile, lane, row)
        return carry

    lax.fori_loop(0, 2 * BOX, fill, 0)
    table_ref[2 * BOX] = jnp.zeros((BOX, SIDE), F32)
    for index in range(2 * PLANES):
        padded[index, 0:SIDE, :] = wave_ref[index]
        padded[index, SIDE:PAD, :] = wave_ref[index, 0:BOX, :]
    sums[...] = jnp.zeros_like(sums)
    inner = lane & (BOX - 1)

    def atom_step(atom, carry):
        depth, start_y, start_z, touched = atom_place(first_ref, centres_ref, atom)

        @pl.when(touched)
        def _():
            kind = species_ref[atom]
            picks = (inner + start_z) & (SIDE - 1)
            totals = [jnp.zeros((8, SIDE), F32), jnp.zeros((8, SIDE), F32)]
            for plane in range(PLANES):
                index = table_row(depth, plane, kind)
                for half in range(2):
                    weights = table_ref[index, half * 8 : half * 8 + 8, :]
                    for part in range(2):
                        values = padded[part * PLANES + plane, pl.ds(start_y + half * 8, 8), :]
                        values = jnp.take_along_axis(values, picks, axis=1)
                        totals[part] = totals[part] + values * weights
            for part in range(2):
                sums[part, pl.ds(atom, 1), :] = jnp.sum(totals[part], axis=0, keepdims=True)

        return carry

    lax.fori_loop(0, SIDE, atom_step, 0)
    group_row = lax.broadcasted_iota(jnp.int32, (NPROJ, SIDE), 0)
    group_lane = lax.broadcasted_iota(jnp.int32, (NPROJ, SIDE), 1)
    groups = (group_lane >> 4 == group_row).astype(F32)
    for part in range(2):
        coef_ref[part * 8 : part * 8 + 8, :] = lax.dot_general(
            groups, sums[part], (((1,), (1,)), ((), ())), precision=highest, preferred_element_type=F32
        )


def spread_kernel(
    first_ref, centres_ref, species_ref, coef_ref, coupling_ref, table_ref, local_ref, out_ref, padded, scaled
):
    lane = lax.broadcasted_iota(jnp.int32, (8, SIDE), 1)
    groups = (lane >> 4 == lax.broadcasted_iota(jnp.int32, (8, SIDE), 0)).astype(F32)
    for kind in range(2):
        mixing = lax.dot_general(
            coupling_ref[kind], groups, (((0,), (0,)), ((), ())), precision=highest, preferred_element_type=F32
        )
        for part in range(2):
            scaled[kind, part] = lax.dot_general(
                coef_ref[part * 8 : part * 8 + 8, :],
                mixing,
                (((0,), (0,)), ((), ())),
                precision=highest,
                preferred_element_type=F32,
            )
    for index in range(2 * PLANES):
        padded[index, 0:SIDE, :] = local_ref[index]
        padded[index, SIDE:PAD, :] = jnp.zeros((BOX, SIDE), F32)

    def atom_step(atom, carry):
        depth, start_y, start_z, touched = atom_place(first_ref, centres_ref, atom)

        @pl.when(touched)
        def _():
            kind = species_ref[atom]
            inside = ((lane - start_z) & (SIDE - 1)) < BOX
            factors = [scaled[kind, part, pl.ds(atom, 1), :] for part in range(2)]
            for plane in range(PLANES):
                index = table_row(depth, plane, kind)
                for half in range(2):
                    weights = table_ref[index, half * 8 : half * 8 + 8, :]
                    for part in range(2):
                        values = weights * factors[part]
                        values = values + pltpu.roll(values, 64, 1)
                        values = values + pltpu.roll(values, 32, 1)
                        values = values + pltpu.roll(values, 16, 1)
                        values = jnp.where(inside, pltpu.roll(values, start_z, 1), 0.0)
                        rows = pl.ds(start_y + half * 8, 8)
                        where = part * PLANES + plane
                        padded[where, rows, :] = padded[where, rows, :] + values

        return carry

    lax.fori_loop(0, SIDE, atom_step, 0)
    for index in range(2 * PLANES):
        out_ref[index, 0:BOX, :] = padded[index, 0:BOX, :] + padded[index, SIDE:PAD, :]
        out_ref[index, BOX:SIDE, :] = padded[index, BOX:SIDE, :]


def local_kernel(wave_ref, potential_ref, high_ref, low_ref, out_ref):
    high = high_ref[...]
    low = low_ref[...]
    for index in range(2 * PLANES):
        value = wave_ref[index]
        out_ref[index] = (
            times_right(value, high, low) + times_left(high, low, value) + potential_ref[index % PLANES] * value
        )


def depth_kernel(value_ref, high_ref, low_ref, out_ref):
    high = high_ref[...]
    low = low_ref[...]
    for row in range(8):
        out_ref[:, row, :] = times_left(high, low, value_ref[:, row, :])


def final_kernel(local_ref, depth_ref, out_ref):
    half_step = 0.5 * time_step
    for plane in range(PLANES):
        out_ref[0, plane] = half_step * (local_ref[1, plane] + depth_ref[1, :, plane])
        out_ref[1, plane] = -half_step * (local_ref[0, plane] + depth_ref[0, :, plane])


def per_device(wave, potential, occupations, centres, species, projectors, coupling):
    vmem, smem = whole(), whole(pltpu.SMEM)
    high, low = kinetic_halves(SIDE)
    blocks = SIDE // 8
    first_plane = jnp.reshape(lax.axis_index("grid") * PLANES, (1,)).astype(jnp.int32)
    tiles = wave.reshape(2, PLANES, blocks, 8, SIDE)
    planes = wave.reshape(2 * PLANES, SIDE, SIDE)
    table_in = projectors.reshape(2 * BOX, NPROJ, BOX * BOX)

    sent = call(pack_kernel, shape(2, blocks, PLANES, 8, SIDE), [vmem], name="pack")(tiles)
    columns = lax.all_to_all(sent.reshape(2 * blocks, PLANES, 8, SIDE), "grid", 0, 0, tiled=True)

    coef, table = call(
        project_kernel,
        (shape(2 * NPROJ, SIDE), shape(2 * BOX + 1, BOX, SIDE)),
        [smem, smem, smem, vmem, vmem],
        [pltpu.VMEM((2 * PLANES, PAD, SIDE), F32), pltpu.VMEM((2, SIDE, SIDE), F32)],
        name="project",
    )(first_plane, centres, species, planes, table_in)
    coef = coef + permuted(coef, "grid", lambda place: place ^ 1)
    coef = coef + permuted(coef, "grid", lambda place: place ^ 2)
    coef = coef + permuted(coef, "grid", lambda place: place + 4) + permuted(coef, "grid", lambda place: place - 4)

    local = call(local_kernel, shape(2 * PLANES, SIDE, SIDE), [vmem] * 4, name="local")(planes, potential, high, low)

    terms = call(density_kernel, shape(2, 2, 2, PLANES, 16, SIDE), [smem, vmem], name="density")(
        occupations, wave.reshape(2, PLANES, SIDE, SIDE)
    )
    place = lax.axis_index("orb")
    for bit in (2, 4, 1):
        mine = (place // bit) % 2
        kept = lax.dynamic_index_in_dim(terms, mine, 0, keepdims=False)
        given = lax.dynamic_index_in_dim(terms, 1 - mine, 0, keepdims=False)
        terms = kept + permuted(given, "orb", lambda source: source ^ bit)
    density = terms

    depth = call(depth_kernel, shape(SIDE, 8, SIDE), [vmem] * 3, name="depth")(
        columns.reshape(SIDE, 8, SIDE), high, low
    )
    returned = lax.all_to_all(depth.reshape(2 * blocks, PLANES, 8, SIDE), "grid", 0, 0, tiled=True)

    total = call(
        spread_kernel,
        shape(2 * PLANES, SIDE, SIDE),
        [smem, smem, smem, vmem, vmem, vmem, vmem],
        [pltpu.VMEM((2 * PLANES, PAD, SIDE), F32), pltpu.VMEM((2, 2, SIDE, SIDE), F32)],
        name="spread",
    )(first_plane, centres, species, coef, coupling, table, local)
    update = call(final_kernel, shape(2, PLANES, blocks, 8, SIDE), [vmem] * 2, name="final")(
        total.reshape(2, PLANES, blocks, 8, SIDE), returned.reshape(2, blocks, PLANES, 8, SIDE)
    )
    return (update.reshape(wave.shape), density)


def solution(mesh):
    placed = (
        P(None, "orb", "grid", None, None),
        P("grid", None, None),
        P("orb"),
        P(),
        P(),
        P(),
        P(),
    )
    return jax.shard_map(
        per_device,
        mesh=mesh,
        in_specs=placed,
        out_specs=(P(None, "orb", "grid", None, None), P("grid", "orb", None)),
        check_vma=False,
    )
```

```python
import math

import jax
import jax.numpy as jnp
import numpy as np
from jax import lax
from jax.experimental import pallas as pl
from jax.experimental.pallas import tpu as pltpu
from jax.sharding import PartitionSpec as P


spacing = 0.32
time_step = 0.1
highest = lax.Precision.HIGHEST

SIDE = 128
BOX = 16
NPROJ = 8
PLANES = 4
PAD = SIDE + BOX
GROUP = 4
F32 = jnp.float32
BF16 = jnp.bfloat16


def permuted(value, axis, target):
    count = lax.axis_size(axis)
    return lax.ppermute(value, axis, [(source, target(source) % count) for source in range(count)])


def kinetic_matrix(extent):
    counts = np.arange(extent)
    signed = np.where(counts < extent // 2, counts, counts - extent)
    waves = signed * (2.0 * math.pi / (extent * spacing))
    angles = (counts[:, None] * counts[None, :] % extent) * (2.0 * math.pi / extent)
    column = (np.cos(angles) * (0.5 * waves**2)[None, :]).sum(axis=1) / extent
    return column[(counts[:, None] - counts[None, :]) % extent]


def kinetic_halves(extent):
    matrix = kinetic_matrix(extent).astype(np.float32)
    high = matrix.astype(BF16)
    low = (matrix - high.astype(np.float32)).astype(BF16)
    row = np.concatenate([high, low], axis=1)
    return jnp.asarray(np.concatenate([row, row], axis=0))


def halves(value):
    high = value.astype(BF16)
    return high, (value - high.astype(F32)).astype(BF16)


def times_right(value, wide):
    product = jnp.dot(jnp.concatenate(halves(value), axis=1), wide, preferred_element_type=F32)
    return product[:, :SIDE] + product[:, SIDE:]


def times_left(pair, value):
    row = jnp.concatenate(halves(value), axis=1)
    product = jnp.dot(pair, jnp.concatenate([row, row], axis=0), preferred_element_type=F32)
    return product[:, :SIDE] + product[:, SIDE:]


def whole(memory=pltpu.VMEM):
    return pl.BlockSpec(memory_space=memory)


def call(kernel, out_shape, specs, scratch=(), outs=None, flops=1000000, moved=1000000):
    return pl.pallas_call(
        kernel,
        out_shape=out_shape,
        in_specs=specs,
        out_specs=jax.tree.map(lambda _: whole(), out_shape) if outs is None else outs,
        scratch_shapes=list(scratch),
        compiler_params=pltpu.CompilerParams(vmem_limit_bytes=12 * 1024 * 1024),
        cost_estimate=pl.CostEstimate(flops=flops, bytes_accessed=moved, transcendentals=0),
    )


def shape(*dims):
    return jax.ShapeDtypeStruct(dims, F32)


def density_kernel(occupation_ref, wave_ref, out_ref):
    occupation = occupation_ref[0]
    for plane in range(PLANES):
        real_part = wave_ref[0, plane]
        imag_part = wave_ref[1, plane]
        term = occupation * (real_part * real_part + imag_part * imag_part)
        for share in range(8):
            high, middle, low = share // 4, share // 2 % 2, share % 2
            out_ref[middle, high, low, plane] = term[share * 16 : share * 16 + 16]


def swap_blocks(tile, lane, row):
    for bit in (1, 2, 4):
        row_set = (row & bit) != 0
        lane_set = ((lane >> 4) & bit) != 0
        up = pltpu.roll(pltpu.roll(tile, 8 - bit, 0), 16 * bit, 1)
        down = pltpu.roll(pltpu.roll(tile, bit, 0), SIDE - 16 * bit, 1)
        tile = jnp.where(row_set == lane_set, tile, jnp.where(lane_set, up, down))
    return tile


def atom_place(first_ref, centres_ref, atom):
    depth = (first_ref[0] - centres_ref[0, atom] + (BOX // 2 + SIDE)) & (SIDE - 1)
    start_y = (centres_ref[1, atom] + (SIDE - BOX // 2)) & (SIDE - 1)
    start_z = (centres_ref[2, atom] + (SIDE - BOX // 2)) & (SIDE - 1)
    touched = ((depth + (PLANES - 1)) & (SIDE - 1)) < BOX + PLANES - 1
    return depth, start_y, start_z, touched


def table_row(depth, plane, kind):
    slot = (depth + plane) & (SIDE - 1)
    return jnp.where(slot < BOX, kind * BOX + slot, 2 * BOX)


def project_kernel(
    first_ref, centres_ref, species_ref, wave_ref, projectors_ref, coef_ref, table_ref, listed_ref, padded, sums
):
    lane = lax.broadcasted_iota(jnp.int32, (8, SIDE), 1)
    row = lax.broadcasted_iota(jnp.int32, (8, SIDE), 0)
    for index in range(2 * PLANES):
        padded[index, 0:SIDE, :] = wave_ref[index]
        padded[index, SIDE:PAD, :] = wave_ref[index, 0:BOX, :]
    sums[...] = jnp.zeros_like(sums)

    def list_step(atom, count):
        touched = atom_place(first_ref, centres_ref, atom)[3]
        listed_ref[count] = atom
        return count + touched.astype(jnp.int32)

    count = lax.fori_loop(0, SIDE, list_step, 0, unroll=8)
    listed_ref[SIDE + GROUP] = count
    for extra in range(GROUP):
        listed_ref[count + extra] = SIDE

    for index in range(2 * BOX):
        for half in range(2):
            tile = projectors_ref[index, :, half * SIDE : (half + 1) * SIDE]
            table_ref[index, half * 8 : half * 8 + 8, :] = swap_blocks(tile, lane, row)
    table_ref[2 * BOX] = jnp.zeros((BOX, SIDE), F32)
    inner = lane & (BOX - 1)

    def group_step(step, carry):
        for offset in range(GROUP):
            listed = listed_ref[step * GROUP + offset]
            atom = jnp.minimum(listed, SIDE - 1)
            depth, start_y, start_z, _ = atom_place(first_ref, centres_ref, atom)
            kind = species_ref[atom]
            picks = (inner + start_z) & (SIDE - 1)
            totals = [jnp.zeros((8, SIDE), F32), jnp.zeros((8, SIDE), F32)]
            for plane in range(PLANES):
                index = table_row(depth, plane, kind)
                for half in range(2):
                    weights = table_ref[index, half * 8 : half * 8 + 8, :]
                    for part in range(2):
                        values = padded[part * PLANES + plane, pl.ds(start_y + half * 8, 8), :]
                        values = jnp.take_along_axis(values, picks, axis=1)
                        totals[part] = totals[part] + values * weights
            for part in range(2):
                sums[part, pl.ds(listed, 1), :] = jnp.sum(totals[part], axis=0, keepdims=True)
        return carry

    lax.fori_loop(0, (count + (GROUP - 1)) // GROUP, group_step, 0)
    group_row = lax.broadcasted_iota(jnp.int32, (NPROJ, SIDE), 0)
    group_lane = lax.broadcasted_iota(jnp.int32, (NPROJ, SIDE), 1)
    groups = (group_lane >> 4 == group_row).astype(F32)
    for part in range(2):
        coef_ref[part * 8 : part * 8 + 8, :] = lax.dot_general(
            groups,
            sums[part, 0:SIDE, :],
            (((1,), (1,)), ((), ())),
            precision=highest,
            preferred_element_type=F32,
        )


def spread_kernel(
    first_ref,
    centres_ref,
    species_ref,
    listed_ref,
    coef_ref,
    coupling_ref,
    table_ref,
    local_ref,
    out_ref,
    padded,
    scaled,
):
    lane = lax.broadcasted_iota(jnp.int32, (8, SIDE), 1)
    groups = (lane >> 4 == lax.broadcasted_iota(jnp.int32, (8, SIDE), 0)).astype(F32)
    for kind in range(2):
        mixing = lax.dot_general(
            coupling_ref[kind], groups, (((0,), (0,)), ((), ())), precision=highest, preferred_element_type=F32
        )
        for part in range(2):
            scaled[kind, part] = lax.dot_general(
                coef_ref[part * 8 : part * 8 + 8, :],
                mixing,
                (((0,), (0,)), ((), ())),
                precision=highest,
                preferred_element_type=F32,
            )
    for index in range(2 * PLANES):
        padded[index, 0:SIDE, :] = local_ref[index]
        padded[index, SIDE:PAD, :] = jnp.zeros((BOX, SIDE), F32)

    def group_step(step, carry):
        for offset in range(GROUP):
            listed = listed_ref[step * GROUP + offset]
            atom = jnp.minimum(listed, SIDE - 1)
            depth, start_y, start_z, _ = atom_place(first_ref, centres_ref, atom)
            kind = species_ref[atom]
            inside = ((lane - start_z) & (SIDE - 1)) < jnp.where(listed < SIDE, BOX, 0)
            factors = [scaled[kind, part, pl.ds(atom, 1), :] for part in range(2)]
            added = []
            for plane in range(PLANES):
                index = table_row(depth, plane, kind)
                for half in range(2):
                    weights = table_ref[index, half * 8 : half * 8 + 8, :]
                    for part in range(2):
                        values = weights * factors[part]
                        values = values + pltpu.roll(values, 64, 1)
                        values = values + pltpu.roll(values, 32, 1)
                        values = values + pltpu.roll(values, 16, 1)
                        values = jnp.where(inside, pltpu.roll(values, start_z, 1), 0.0)
                        added.append((part * PLANES + plane, start_y + half * 8, values))
            for where, start, values in added:
                padded[where, pl.ds(start, 8), :] = padded[where, pl.ds(start, 8), :] + values
        return carry

    lax.fori_loop(0, (listed_ref[SIDE + GROUP] + (GROUP - 1)) // GROUP, group_step, 0)
    for index in range(2 * PLANES):
        out_ref[index, 0:BOX, :] = padded[index, 0:BOX, :] + padded[index, SIDE:PAD, :]
        out_ref[index, BOX:SIDE, :] = padded[index, BOX:SIDE, :]


def local_kernel(wave_ref, potential_ref, wide_ref, out_ref):
    wide = wide_ref[...]
    pair = wide_ref[0:SIDE, :]
    for index in range(2 * PLANES):
        value = wave_ref[index]
        out_ref[index] = times_right(value, wide) + times_left(pair, value) + potential_ref[index % PLANES] * value


def depth_kernel(value_ref, wide_ref, out_ref):
    pair = wide_ref[0:SIDE, :]
    for row in range(8):
        out_ref[:, row, :] = times_left(pair, value_ref[:, row, :])


def final_kernel(local_ref, depth_ref, out_ref):
    half_step = 0.5 * time_step
    for plane in range(PLANES):
        out_ref[0, plane] = half_step * (local_ref[1, plane] + depth_ref[1, :, plane])
        out_ref[1, plane] = -half_step * (local_ref[0, plane] + depth_ref[0, :, plane])


def whole_step(wave, potential, occupations, centres, species, projectors, coupling):
    vmem, smem = whole(), whole(pltpu.SMEM)
    wide = kinetic_halves(SIDE)
    blocks = SIDE // 8
    first_plane = jnp.reshape(lax.axis_index("grid") * PLANES, (1,)).astype(jnp.int32)
    tiles = wave.reshape(2, PLANES, blocks, 8, SIDE)
    planes = wave.reshape(2 * PLANES, SIDE, SIDE)
    table_in = projectors.reshape(2 * BOX, NPROJ, BOX * BOX)

    sent = jnp.transpose(tiles, (0, 2, 1, 3, 4)).reshape(2 * blocks, PLANES, 8, SIDE)
    columns = lax.all_to_all(sent, "grid", 0, 0, tiled=True)

    terms = call(density_kernel, shape(2, 2, 2, PLANES, 16, SIDE), [smem, vmem])(
        occupations, wave.reshape(2, PLANES, SIDE, SIDE)
    )
    coef, table, listed = call(
        project_kernel,
        (shape(2 * NPROJ, SIDE), shape(2 * BOX + 1, BOX, SIDE), jax.ShapeDtypeStruct((SIDE + GROUP + 1,), jnp.int32)),
        [smem, smem, smem, vmem, vmem],
        [pltpu.VMEM((2 * PLANES, PAD, SIDE), F32), pltpu.VMEM((2, SIDE + 8, SIDE), F32)],
        outs=(vmem, vmem, smem),
    )(first_plane, centres, species, planes, table_in)
    coef = coef + permuted(coef, "grid", lambda place: place ^ 1)
    coef = coef + permuted(coef, "grid", lambda place: place ^ 2)
    above = permuted(coef, "grid", lambda place: place + 4)
    below = permuted(coef, "grid", lambda place: place - 4)
    total_coef = coef + above + below

    local = call(local_kernel, shape(2 * PLANES, SIDE, SIDE), [vmem] * 3)(planes, potential, wide)

    place = lax.axis_index("orb")
    for bit in (2, 4, 1):
        mine = (place // bit) % 2
        kept = lax.dynamic_index_in_dim(terms, mine, 0, keepdims=False)
        given = lax.dynamic_index_in_dim(terms, 1 - mine, 0, keepdims=False)
        terms = kept + permuted(given, "orb", lambda source: source ^ bit)
    density = terms

    depth = call(depth_kernel, shape(SIDE, 8, SIDE), [vmem] * 2)(
        columns.reshape(SIDE, 8, SIDE), wide
    )
    returned = lax.all_to_all(depth.reshape(2 * blocks, PLANES, 8, SIDE), "grid", 0, 0, tiled=True)

    total = call(
        spread_kernel,
        shape(2 * PLANES, SIDE, SIDE),
        [smem, smem, smem, smem, vmem, vmem, vmem, vmem],
        [pltpu.VMEM((2 * PLANES, PAD, SIDE), F32), pltpu.VMEM((2, 2, SIDE, SIDE), F32)],
    )(first_plane, centres, species, listed, total_coef, coupling, table, local)
    update = call(final_kernel, shape(2, PLANES, blocks, 8, SIDE), [vmem] * 2)(
        total.reshape(2, PLANES, blocks, 8, SIDE), returned.reshape(2, blocks, PLANES, 8, SIDE)
    )
    return (update.reshape(wave.shape), density)


def solution(mesh):
    placed = (
        P(None, "orb", "grid", None, None),
        P("grid", None, None),
        P("orb"),
        P(),
        P(),
        P(),
        P(),
    )
    return jax.shard_map(
        whole_step,
        mesh=mesh,
        in_specs=placed,
        out_specs=(P(None, "orb", "grid", None, None), P("grid", "orb", None)),
        check_vma=False,
    )
```

```python
import math

import jax
import jax.numpy as jnp
import numpy as np
from jax import lax
from jax.experimental import pallas as pl
from jax.experimental.pallas import tpu as pltpu
from jax.sharding import PartitionSpec as P


spacing = 0.32
time_step = 0.1
highest = lax.Precision.HIGHEST

SIDE = 128
BOX = 16
NPROJ = 8
PLANES = 4
PAD = SIDE + BOX
GROUP = 4
F32 = jnp.float32
BF16 = jnp.bfloat16


def permuted(value, axis, target):
    count = lax.axis_size(axis)
    return lax.ppermute(value, axis, [(source, target(source) % count) for source in range(count)])


def kinetic_matrix(extent):
    counts = np.arange(extent)
    signed = np.where(counts < extent // 2, counts, counts - extent)
    waves = signed * (2.0 * math.pi / (extent * spacing))
    angles = (counts[:, None] * counts[None, :] % extent) * (2.0 * math.pi / extent)
    column = (np.cos(angles) * (0.5 * waves**2)[None, :]).sum(axis=1) / extent
    return column[(counts[:, None] - counts[None, :]) % extent]


def kinetic_halves(extent):
    matrix = kinetic_matrix(extent).astype(np.float32)
    high = matrix.astype(BF16)
    low = (matrix - high.astype(np.float32)).astype(BF16)
    row = np.concatenate([high, low], axis=1)
    return jnp.asarray(np.concatenate([row, row], axis=0))


def halves(value):
    high = value.astype(BF16)
    return high, (value - high.astype(F32)).astype(BF16)


def times_right(value, wide):
    product = jnp.dot(jnp.concatenate(halves(value), axis=1), wide, preferred_element_type=F32)
    return product[:, :SIDE] + product[:, SIDE:]


def times_left(pair, value):
    row = jnp.concatenate(halves(value), axis=1)
    product = jnp.dot(pair, jnp.concatenate([row, row], axis=0), preferred_element_type=F32)
    return product[:, :SIDE] + product[:, SIDE:]


def whole(memory=pltpu.VMEM):
    return pl.BlockSpec(memory_space=memory)


def call(kernel, out_shape, specs, scratch=(), outs=None, flops=1000000, moved=1000000):
    return pl.pallas_call(
        kernel,
        out_shape=out_shape,
        in_specs=specs,
        out_specs=jax.tree.map(lambda _: whole(), out_shape) if outs is None else outs,
        scratch_shapes=list(scratch),
        compiler_params=pltpu.CompilerParams(vmem_limit_bytes=12 * 1024 * 1024),
        cost_estimate=pl.CostEstimate(flops=flops, bytes_accessed=moved, transcendentals=0),
    )


def shape(*dims):
    return jax.ShapeDtypeStruct(dims, F32)


def density_kernel(occupation_ref, wave_ref, out_ref):
    occupation = occupation_ref[0]
    for plane in range(PLANES):
        real_part = wave_ref[0, plane]
        imag_part = wave_ref[1, plane]
        term = occupation * (real_part * real_part + imag_part * imag_part)
        for share in range(8):
            high, middle, low = share // 4, share // 2 % 2, share % 2
            out_ref[middle, high, low, plane] = term[share * 16 : share * 16 + 16]


def swap_blocks(tile, lane, row):
    for bit in (1, 2, 4):
        row_set = (row & bit) != 0
        lane_set = ((lane >> 4) & bit) != 0
        up = pltpu.roll(pltpu.roll(tile, 8 - bit, 0), 16 * bit, 1)
        down = pltpu.roll(pltpu.roll(tile, bit, 0), SIDE - 16 * bit, 1)
        tile = jnp.where(row_set == lane_set, tile, jnp.where(lane_set, up, down))
    return tile


def atom_place(first_ref, centres_ref, atom):
    depth = (first_ref[0] - centres_ref[0, atom] + (BOX // 2 + SIDE)) & (SIDE - 1)
    start_y = (centres_ref[1, atom] + (SIDE - BOX // 2)) & (SIDE - 1)
    start_z = (centres_ref[2, atom] + (SIDE - BOX // 2)) & (SIDE - 1)
    touched = ((depth + (PLANES - 1)) & (SIDE - 1)) < BOX + PLANES - 1
    return depth, start_y, start_z, touched


def table_row(depth, plane, kind):
    slot = (depth + plane) & (SIDE - 1)
    return jnp.where(slot < BOX, kind * BOX + slot, 2 * BOX)


def project_kernel(
    first_ref, centres_ref, species_ref, wave_ref, projectors_ref, coef_ref, table_ref, listed_ref, padded, sums
):
    lane = lax.broadcasted_iota(jnp.int32, (8, SIDE), 1)
    row = lax.broadcasted_iota(jnp.int32, (8, SIDE), 0)
    for index in range(2 * PLANES):
        padded[index, 0:SIDE, :] = wave_ref[index]
        padded[index, SIDE:PAD, :] = wave_ref[index, 0:BOX, :]
    sums[...] = jnp.zeros_like(sums)

    def list_step(atom, count):
        touched = atom_place(first_ref, centres_ref, atom)[3]
        listed_ref[count] = atom
        return count + touched.astype(jnp.int32)

    count = lax.fori_loop(0, SIDE, list_step, 0, unroll=8)
    listed_ref[SIDE + GROUP] = count
    for extra in range(GROUP):
        listed_ref[count + extra] = SIDE

    for index in range(2 * BOX):
        for half in range(2):
            tile = projectors_ref[index, :, half * SIDE : (half + 1) * SIDE]
            table_ref[index, half * 8 : half * 8 + 8, :] = swap_blocks(tile, lane, row)
    table_ref[2 * BOX] = jnp.zeros((BOX, SIDE), F32)
    inner = lane & (BOX - 1)

    def group_step(step, carry):
        for offset in range(GROUP):
            listed = listed_ref[step * GROUP + offset]
            atom = jnp.minimum(listed, SIDE - 1)
            depth, start_y, start_z, _ = atom_place(first_ref, centres_ref, atom)
            kind = species_ref[atom]
            picks = (inner + start_z) & (SIDE - 1)
            totals = [jnp.zeros((8, SIDE), F32), jnp.zeros((8, SIDE), F32)]
            for plane in range(PLANES):
                index = table_row(depth, plane, kind)
                for half in range(2):
                    weights = table_ref[index, half * 8 : half * 8 + 8, :]
                    for part in range(2):
                        values = padded[part * PLANES + plane, pl.ds(start_y + half * 8, 8), :]
                        values = jnp.take_along_axis(values, picks, axis=1)
                        totals[part] = totals[part] + values * weights
            for part in range(2):
                sums[part, pl.ds(listed, 1), :] = jnp.sum(totals[part], axis=0, keepdims=True)
        return carry

    lax.fori_loop(0, (count + (GROUP - 1)) // GROUP, group_step, 0)
    groups = ((lax.broadcasted_iota(jnp.int32, (NPROJ, 2 * SIDE), 1) >> 4) & (NPROJ - 1)) == (
        lax.broadcasted_iota(jnp.int32, (NPROJ, 2 * SIDE), 0)
    )
    rows = jnp.concatenate([sums[part, 0:SIDE, :] for part in range(2)], axis=0)
    coef = lax.dot_general(
        groups.astype(F32).astype(BF16),
        jnp.concatenate(halves(rows), axis=1),
        (((1,), (1,)), ((), ())),
        preferred_element_type=F32,
    )
    coef_ref[0:8, :] = coef[:, :SIDE]
    coef_ref[8:16, :] = coef[:, SIDE:]


def spread_kernel(
    first_ref,
    centres_ref,
    species_ref,
    listed_ref,
    coef_ref,
    coupling_ref,
    table_ref,
    local_ref,
    out_ref,
    padded,
    scaled,
):
    lane = lax.broadcasted_iota(jnp.int32, (8, SIDE), 1)
    groups = (lax.broadcasted_iota(jnp.int32, (2 * NPROJ, 2 * SIDE), 1) >> 4) == (
        lax.broadcasted_iota(jnp.int32, (2 * NPROJ, 2 * SIDE), 0)
    )
    mixing = lax.dot_general(
        coupling_ref[...],
        groups.astype(F32),
        (((0,), (0,)), ((), ())),
        precision=highest,
        preferred_element_type=F32,
    )
    scaled[...] = lax.dot_general(
        jnp.concatenate([coef_ref[0:8, :], coef_ref[8:16, :]], axis=1),
        mixing,
        (((0,), (0,)), ((), ())),
        precision=highest,
        preferred_element_type=F32,
    )
    for index in range(2 * PLANES):
        padded[index, 0:SIDE, :] = local_ref[index]
        padded[index, SIDE:PAD, :] = jnp.zeros((BOX, SIDE), F32)

    def group_step(step, carry):
        for offset in range(GROUP):
            listed = listed_ref[step * GROUP + offset]
            atom = jnp.minimum(listed, SIDE - 1)
            depth, start_y, start_z, _ = atom_place(first_ref, centres_ref, atom)
            kind = species_ref[atom]
            inside = ((lane - start_z) & (SIDE - 1)) < jnp.where(listed < SIDE, BOX, 0)
            both = [scaled[pl.ds(part * SIDE + atom, 1), :] for part in range(2)]
            factors = [jnp.where(kind == 0, pair[:, :SIDE], pair[:, SIDE:]) for pair in both]
            added = []
            for plane in range(PLANES):
                index = table_row(depth, plane, kind)
                for half in range(2):
                    weights = table_ref[index, half * 8 : half * 8 + 8, :]
                    for part in range(2):
                        values = weights * factors[part]
                        values = values + pltpu.roll(values, 64, 1)
                        values = values + pltpu.roll(values, 32, 1)
                        values = values + pltpu.roll(values, 16, 1)
                        values = jnp.where(inside, pltpu.roll(values, start_z, 1), 0.0)
                        added.append((part * PLANES + plane, start_y + half * 8, values))
            for where, start, values in added:
                padded[where, pl.ds(start, 8), :] = padded[where, pl.ds(start, 8), :] + values
        return carry

    lax.fori_loop(0, (listed_ref[SIDE + GROUP] + (GROUP - 1)) // GROUP, group_step, 0)
    for index in range(2 * PLANES):
        out_ref[index, 0:BOX, :] = padded[index, 0:BOX, :] + padded[index, SIDE:PAD, :]
        out_ref[index, BOX:SIDE, :] = padded[index, BOX:SIDE, :]


def local_kernel(wave_ref, potential_ref, wide_ref, out_ref):
    wide = wide_ref[...]
    pair = wide_ref[0:SIDE, :]
    for index in range(2 * PLANES):
        value = wave_ref[index]
        out_ref[index] = times_right(value, wide) + times_left(pair, value) + potential_ref[index % PLANES] * value


def depth_kernel(value_ref, wide_ref, out_ref):
    pair = wide_ref[0:SIDE, :]
    for row in range(8):
        out_ref[:, row, :] = times_left(pair, value_ref[:, row, :])


def final_kernel(local_ref, depth_ref, out_ref):
    half_step = 0.5 * time_step
    for plane in range(PLANES):
        out_ref[0, plane] = half_step * (local_ref[1, plane] + depth_ref[1, :, plane])
        out_ref[1, plane] = -half_step * (local_ref[0, plane] + depth_ref[0, :, plane])


def whole_step(wave, potential, occupations, centres, species, projectors, coupling):
    vmem, smem = whole(), whole(pltpu.SMEM)
    wide = kinetic_halves(SIDE)
    blocks = SIDE // 8
    first_plane = jnp.reshape(lax.axis_index("grid") * PLANES, (1,)).astype(jnp.int32)
    tiles = wave.reshape(2, PLANES, blocks, 8, SIDE)
    planes = wave.reshape(2 * PLANES, SIDE, SIDE)
    table_in = projectors.reshape(2 * BOX, NPROJ, BOX * BOX)

    sent = jnp.transpose(tiles, (0, 2, 1, 3, 4)).reshape(2 * blocks, PLANES, 8, SIDE)
    columns = lax.all_to_all(sent, "grid", 0, 0, tiled=True)

    terms = call(density_kernel, shape(2, 2, 2, PLANES, 16, SIDE), [smem, vmem])(
        occupations, wave.reshape(2, PLANES, SIDE, SIDE)
    )
    coef, table, listed = call(
        project_kernel,
        (shape(2 * NPROJ, SIDE), shape(2 * BOX + 1, BOX, SIDE), jax.ShapeDtypeStruct((SIDE + GROUP + 1,), jnp.int32)),
        [smem, smem, smem, vmem, vmem],
        [pltpu.VMEM((2 * PLANES, PAD, SIDE), F32), pltpu.VMEM((2, SIDE + 8, SIDE), F32)],
        outs=(vmem, vmem, smem),
    )(first_plane, centres, species, planes, table_in)
    coef = coef + permuted(coef, "grid", lambda place: place ^ 1)
    coef = coef + permuted(coef, "grid", lambda place: place ^ 2)
    above = permuted(coef, "grid", lambda place: place + 4)
    below = permuted(coef, "grid", lambda place: place - 4)
    total_coef = coef + above + below

    local = call(local_kernel, shape(2 * PLANES, SIDE, SIDE), [vmem] * 3)(planes, potential, wide)

    place = lax.axis_index("orb")
    for bit in (2, 4, 1):
        mine = (place // bit) % 2
        kept = lax.dynamic_index_in_dim(terms, mine, 0, keepdims=False)
        given = lax.dynamic_index_in_dim(terms, 1 - mine, 0, keepdims=False)
        terms = kept + permuted(given, "orb", lambda source: source ^ bit)
    density = terms

    depth = call(depth_kernel, shape(SIDE, 8, SIDE), [vmem] * 2)(
        columns.reshape(SIDE, 8, SIDE), wide
    )
    returned = lax.all_to_all(depth.reshape(2 * blocks, PLANES, 8, SIDE), "grid", 0, 0, tiled=True)

    total = call(
        spread_kernel,
        shape(2 * PLANES, SIDE, SIDE),
        [smem, smem, smem, smem, vmem, vmem, vmem, vmem],
        [pltpu.VMEM((2 * PLANES, PAD, SIDE), F32), pltpu.VMEM((2 * SIDE, 2 * SIDE), F32)],
    )(first_plane, centres, species, listed, total_coef, coupling.reshape(2 * NPROJ, NPROJ), table, local)
    update = call(final_kernel, shape(2, PLANES, blocks, 8, SIDE), [vmem] * 2)(
        total.reshape(2, PLANES, blocks, 8, SIDE), returned.reshape(2, blocks, PLANES, 8, SIDE)
    )
    return (update.reshape(wave.shape), density)


def solution(mesh):
    placed = (
        P(None, "orb", "grid", None, None),
        P("grid", None, None),
        P("orb"),
        P(),
        P(),
        P(),
        P(),
    )
    return jax.shard_map(
        whole_step,
        mesh=mesh,
        in_specs=placed,
        out_specs=(P(None, "orb", "grid", None, None), P("grid", "orb", None)),
        check_vma=False,
    )
```

```python
import math

import jax
import jax.numpy as jnp
import numpy as np
from jax import lax
from jax.experimental import pallas as pl
from jax.experimental.pallas import tpu as pltpu
from jax.sharding import PartitionSpec as P


spacing = 0.32
time_step = 0.1
highest = lax.Precision.HIGHEST

SIDE = 128
BOX = 16
NPROJ = 8
PLANES = 4
PAD = SIDE + BOX
GROUP = 4
FIELD = 136
COUNT = 5 * FIELD
F32 = jnp.float32
BF16 = jnp.bfloat16


def permuted(value, axis, target):
    count = lax.axis_size(axis)
    return lax.ppermute(value, axis, [(source, target(source) % count) for source in range(count)])


def kinetic_matrix(extent):
    counts = np.arange(extent)
    signed = np.where(counts < extent // 2, counts, counts - extent)
    waves = signed * (2.0 * math.pi / (extent * spacing))
    angles = (counts[:, None] * counts[None, :] % extent) * (2.0 * math.pi / extent)
    column = (np.cos(angles) * (0.5 * waves**2)[None, :]).sum(axis=1) / extent
    return column[(counts[:, None] - counts[None, :]) % extent]


def kinetic_halves(extent):
    matrix = kinetic_matrix(extent).astype(np.float32)
    high = matrix.astype(BF16)
    low = (matrix - high.astype(np.float32)).astype(BF16)
    row = np.concatenate([high, low], axis=1)
    return jnp.asarray(np.concatenate([row, row], axis=0))


def halves(value):
    high = value.astype(BF16)
    return high, (value - high.astype(F32)).astype(BF16)


def times_right(value, wide):
    product = jnp.dot(jnp.concatenate(halves(value), axis=1), wide, preferred_element_type=F32)
    return product[:, :SIDE] + product[:, SIDE:]


def times_left(pair, value):
    row = jnp.concatenate(halves(value), axis=1)
    product = jnp.dot(pair, jnp.concatenate([row, row], axis=0), preferred_element_type=F32)
    return product[:, :SIDE] + product[:, SIDE:]


def whole(memory=pltpu.VMEM):
    return pl.BlockSpec(memory_space=memory)


def call(kernel, out_shape, specs, scratch=(), outs=None, flops=1000000, moved=1000000):
    return pl.pallas_call(
        kernel,
        out_shape=out_shape,
        in_specs=specs,
        out_specs=jax.tree.map(lambda _: whole(), out_shape) if outs is None else outs,
        scratch_shapes=list(scratch),
        compiler_params=pltpu.CompilerParams(vmem_limit_bytes=12 * 1024 * 1024),
        cost_estimate=pl.CostEstimate(flops=flops, bytes_accessed=moved, transcendentals=0),
    )


def shape(*dims):
    return jax.ShapeDtypeStruct(dims, F32)


def density_kernel(occupation_ref, wave_ref, out_ref):
    occupation = occupation_ref[0]
    for plane in range(PLANES):
        real_part = wave_ref[0, plane]
        imag_part = wave_ref[1, plane]
        term = occupation * (real_part * real_part + imag_part * imag_part)
        for share in range(8):
            high, middle, low = share // 4, share // 2 % 2, share % 2
            out_ref[middle, high, low, plane] = term[share * 16 : share * 16 + 16]


def swap_blocks(tile, lane, row):
    for bit in (1, 2, 4):
        row_set = (row & bit) != 0
        lane_set = ((lane >> 4) & bit) != 0
        up = pltpu.roll(pltpu.roll(tile, 8 - bit, 0), 16 * bit, 1)
        down = pltpu.roll(pltpu.roll(tile, bit, 0), SIDE - 16 * bit, 1)
        tile = jnp.where(row_set == lane_set, tile, jnp.where(lane_set, up, down))
    return tile


def atom_place(first_plane, centres_ref, atom):
    depth = (first_plane - centres_ref[0, atom] + (BOX // 2 + SIDE)) & (SIDE - 1)
    start_y = (centres_ref[1, atom] + (SIDE - BOX // 2)) & (SIDE - 1)
    start_z = (centres_ref[2, atom] + (SIDE - BOX // 2)) & (SIDE - 1)
    touched = ((depth + (PLANES - 1)) & (SIDE - 1)) < BOX + PLANES - 1
    return depth, start_y, start_z, touched


def table_row(depth, plane, kind):
    slot = (depth + plane) & (SIDE - 1)
    return jnp.where(slot < BOX, kind * BOX + slot, 2 * BOX)


def entry(listed_ref, index):
    return [listed_ref[field * FIELD + index] for field in range(5)]


def group_count(listed_ref):
    return (listed_ref[COUNT] + (GROUP - 1)) // GROUP


def project_kernel(listed_ref, wave_ref, projectors_ref, coef_ref, table_ref, padded, sums):
    lane = lax.broadcasted_iota(jnp.int32, (8, SIDE), 1)
    row = lax.broadcasted_iota(jnp.int32, (8, SIDE), 0)
    for index in range(2 * PLANES):
        padded[index, 0:SIDE, :] = wave_ref[index]
        padded[index, SIDE:PAD, :] = wave_ref[index, 0:BOX, :]
    sums[...] = jnp.zeros_like(sums)

    for index in range(2 * BOX):
        for half in range(2):
            tile = projectors_ref[index, :, half * SIDE : (half + 1) * SIDE]
            table_ref[index, half * 8 : half * 8 + 8, :] = swap_blocks(tile, lane, row)
    table_ref[2 * BOX] = jnp.zeros((BOX, SIDE), F32)
    inner = lane & (BOX - 1)

    def group_step(step, carry):
        for offset in range(GROUP):
            listed, depth, start_y, start_z, kind = entry(listed_ref, step * GROUP + offset)
            picks = (inner + start_z) & (SIDE - 1)
            totals = [jnp.zeros((8, SIDE), F32), jnp.zeros((8, SIDE), F32)]
            for plane in range(PLANES):
                index = table_row(depth, plane, kind)
                for half in range(2):
                    weights = table_ref[index, half * 8 : half * 8 + 8, :]
                    for part in range(2):
                        values = padded[part * PLANES + plane, pl.ds(start_y + half * 8, 8), :]
                        values = jnp.take_along_axis(values, picks, axis=1)
                        totals[part] = totals[part] + values * weights
            for part in range(2):
                sums[part, pl.ds(listed, 1), :] = jnp.sum(totals[part], axis=0, keepdims=True)
        return carry

    lax.fori_loop(0, group_count(listed_ref), group_step, 0)
    groups = ((lax.broadcasted_iota(jnp.int32, (NPROJ, 2 * SIDE), 1) >> 4) & (NPROJ - 1)) == (
        lax.broadcasted_iota(jnp.int32, (NPROJ, 2 * SIDE), 0)
    )
    rows = jnp.concatenate([sums[part, 0:SIDE, :] for part in range(2)], axis=0)
    coef = lax.dot_general(
        groups.astype(F32).astype(BF16),
        jnp.concatenate(halves(rows), axis=1),
        (((1,), (1,)), ((), ())),
        preferred_element_type=F32,
    )
    coef_ref[0:8, :] = coef[:, :SIDE]
    coef_ref[8:16, :] = coef[:, SIDE:]


def spread_kernel(
    listed_ref,
    coef_ref,
    coupling_ref,
    table_ref,
    local_ref,
    out_ref,
    padded,
    scaled,
):
    lane = lax.broadcasted_iota(jnp.int32, (8, SIDE), 1)
    groups = (lax.broadcasted_iota(jnp.int32, (2 * NPROJ, 2 * SIDE), 1) >> 4) == (
        lax.broadcasted_iota(jnp.int32, (2 * NPROJ, 2 * SIDE), 0)
    )
    mixing = lax.dot_general(
        coupling_ref[...],
        groups.astype(F32),
        (((0,), (0,)), ((), ())),
        precision=highest,
        preferred_element_type=F32,
    )
    scaled[...] = lax.dot_general(
        jnp.concatenate([coef_ref[0:8, :], coef_ref[8:16, :]], axis=1),
        mixing,
        (((0,), (0,)), ((), ())),
        precision=highest,
        preferred_element_type=F32,
    )
    for index in range(2 * PLANES):
        padded[index, 0:SIDE, :] = local_ref[index]
        padded[index, SIDE:PAD, :] = jnp.zeros((BOX, SIDE), F32)

    def group_step(step, carry):
        for offset in range(GROUP):
            listed, depth, start_y, start_z, kind = entry(listed_ref, step * GROUP + offset)
            atom = jnp.minimum(listed, SIDE - 1)
            inside = ((lane - start_z) & (SIDE - 1)) < BOX
            both = [scaled[pl.ds(part * SIDE + atom, 1), :] for part in range(2)]
            factors = [jnp.where(kind == 0, pair[:, :SIDE], pair[:, SIDE:]) for pair in both]
            added = []
            for plane in range(PLANES):
                index = table_row(depth, plane, kind)
                for half in range(2):
                    weights = table_ref[index, half * 8 : half * 8 + 8, :]
                    for part in range(2):
                        values = weights * factors[part]
                        values = values + pltpu.roll(values, 64, 1)
                        values = values + pltpu.roll(values, 32, 1)
                        values = values + pltpu.roll(values, 16, 1)
                        values = jnp.where(inside, pltpu.roll(values, start_z, 1), 0.0)
                        added.append((part * PLANES + plane, start_y + half * 8, values))
            for where, start, values in added:
                padded[where, pl.ds(start, 8), :] = padded[where, pl.ds(start, 8), :] + values
        return carry

    lax.fori_loop(0, group_count(listed_ref), group_step, 0)
    for index in range(2 * PLANES):
        out_ref[index, 0:BOX, :] = padded[index, 0:BOX, :] + padded[index, SIDE:PAD, :]
        out_ref[index, BOX:SIDE, :] = padded[index, BOX:SIDE, :]


def local_kernel(wave_ref, potential_ref, wide_ref, out_ref):
    wide = wide_ref[...]
    pair = wide_ref[0:SIDE, :]
    for index in range(2 * PLANES):
        value = wave_ref[index]
        out_ref[index] = times_right(value, wide) + times_left(pair, value) + potential_ref[index % PLANES] * value


def depth_kernel(value_ref, wide_ref, out_ref, rows, sems):
    pair = wide_ref[0:SIDE, :]
    copies = []
    for row in range(8):
        rows[row] = times_left(pair, value_ref[pl.ds(row, SIDE, stride=8), :])
        copies.append(pltpu.make_async_copy(rows.at[row], out_ref.at[:, row, :], sems.at[row]))
        copies[-1].start()
    for copy in copies:
        copy.wait()


def list_atoms(first_plane, centres_ref, species_ref, listed_ref):
    def list_step(atom, count):
        touched = atom_place(first_plane, centres_ref, atom)[3]
        listed_ref[count] = atom
        return count + touched.astype(jnp.int32)

    count = lax.fori_loop(0, SIDE, list_step, 0, unroll=8)
    listed_ref[COUNT] = count

    def detail_step(index, carry):
        atom = listed_ref[index]
        depth, start_y, start_z, _ = atom_place(first_plane, centres_ref, atom)
        for field, value in enumerate((depth, start_y, start_z, species_ref[atom])):
            listed_ref[(field + 1) * FIELD + index] = value
        return carry

    lax.fori_loop(0, count, detail_step, 0)
    for extra in range(GROUP):
        for field, value in enumerate((SIDE, SIDE // 2, 0, 0, 0)):
            listed_ref[field * FIELD + count + extra] = jnp.int32(value)


def pack_kernel(
    first_ref,
    wave_ref,
    centres_ref,
    species_ref,
    out_ref,
    listed_out_ref,
    held,
    centres,
    species,
    listed,
    in_sems,
    out_sems,
    list_sems,
):
    places = [(part, plane) for part in range(2) for plane in range(PLANES)]
    arriving = [
        pltpu.make_async_copy(wave_ref.at[place], held.at[place], in_sems.at[slot]) for slot, place in enumerate(places)
    ]
    leaving = [
        pltpu.make_async_copy(held.at[part, plane], out_ref.at[part, :, plane], out_sems.at[slot])
        for slot, (part, plane) in enumerate(places)
    ]
    tables = [
        pltpu.make_async_copy(centres_ref, centres, list_sems.at[0]),
        pltpu.make_async_copy(species_ref, species, list_sems.at[1]),
    ]
    listing = pltpu.make_async_copy(listed, listed_out_ref, list_sems.at[2])
    for copy in tables + arriving:
        copy.start()
    for first, second in zip(arriving, leaving):
        first.wait()
        second.start()
    for copy in tables:
        copy.wait()
    list_atoms(first_ref[0], centres, species, listed)
    listing.start()
    for copy in leaving:
        copy.wait()
    listing.wait()


def final_kernel(local_ref, depth_ref, out_ref, held, sems):
    half_step = 0.5 * time_step
    copies = []
    for plane in range(PLANES):
        for part, sign in ((0, half_step), (1, -half_step)):
            held[part, plane] = sign * (local_ref[1 - part, plane] + depth_ref[1 - part, :, plane])
            copies.append(
                pltpu.make_async_copy(held.at[part, plane], out_ref.at[part, plane], sems.at[part * PLANES + plane])
            )
            copies[-1].start()
    for copy in copies:
        copy.wait()


def whole_step(wave, potential, occupations, centres, species, projectors, coupling):
    vmem, smem, outside = whole(), whole(pltpu.SMEM), whole(pl.ANY)
    wide = kinetic_halves(SIDE)
    blocks = SIDE // 8
    first_plane = jnp.reshape(lax.axis_index("grid") * PLANES, (1,)).astype(jnp.int32)
    tiles = wave.reshape(2, PLANES, blocks, 8, SIDE)
    planes = wave.reshape(2 * PLANES, SIDE, SIDE)
    table_in = projectors.reshape(2 * BOX, NPROJ, BOX * BOX)

    sent, listed = call(
        pack_kernel,
        (shape(2, blocks, PLANES, 8, SIDE), jax.ShapeDtypeStruct((COUNT + FIELD,), jnp.int32)),
        [smem] + [whole(pltpu.HBM)] * 3,
        [
            pltpu.VMEM((2, PLANES, blocks, 8, SIDE), F32),
            pltpu.SMEM((3, SIDE), jnp.int32),
            pltpu.SMEM((SIDE,), jnp.int32),
            pltpu.SMEM((COUNT + FIELD,), jnp.int32),
            pltpu.SemaphoreType.DMA((2 * PLANES,)),
            pltpu.SemaphoreType.DMA((2 * PLANES,)),
            pltpu.SemaphoreType.DMA((3,)),
        ],
        outs=(outside, outside),
    )(first_plane, *(pltpu.with_memory_space_constraint(value, pltpu.HBM) for value in (tiles, centres, species)))
    sent = sent.reshape(2 * blocks, PLANES, 8, SIDE)
    columns = lax.all_to_all(sent, "grid", 0, 0, tiled=True)

    terms = call(density_kernel, shape(2, 2, 2, PLANES, 16, SIDE), [smem, vmem])(
        occupations, wave.reshape(2, PLANES, SIDE, SIDE)
    )
    coef, table = call(
        project_kernel,
        (shape(2 * NPROJ, SIDE), shape(2 * BOX + 1, BOX, SIDE)),
        [smem, vmem, vmem],
        [pltpu.VMEM((2 * PLANES, PAD, SIDE), F32), pltpu.VMEM((2, SIDE + 8, SIDE), F32)],
    )(listed, planes, table_in)
    coef = coef + permuted(coef, "grid", lambda place: place ^ 1)
    coef = coef + permuted(coef, "grid", lambda place: place ^ 2)
    above = permuted(coef, "grid", lambda place: place + 4)
    below = permuted(coef, "grid", lambda place: place - 4)
    total_coef = coef + above + below

    local = call(local_kernel, shape(2 * PLANES, SIDE, SIDE), [vmem] * 3)(planes, potential, wide)

    place = lax.axis_index("orb")
    for bit in (2, 4, 1):
        mine = (place // bit) % 2
        kept = lax.dynamic_index_in_dim(terms, mine, 0, keepdims=False)
        given = lax.dynamic_index_in_dim(terms, 1 - mine, 0, keepdims=False)
        terms = kept + permuted(given, "orb", lambda source: source ^ bit)
    density = terms

    depth = call(
        depth_kernel,
        shape(SIDE, 8, SIDE),
        [vmem] * 2,
        [pltpu.VMEM((8, SIDE, SIDE), F32), pltpu.SemaphoreType.DMA((8,))],
        outs=outside,
    )(columns.reshape(8 * SIDE, SIDE), wide)
    returned = lax.all_to_all(depth.reshape(2 * blocks, PLANES, 8, SIDE), "grid", 0, 0, tiled=True)

    total = call(
        spread_kernel,
        shape(2 * PLANES, SIDE, SIDE),
        [smem, vmem, vmem, vmem, vmem],
        [pltpu.VMEM((2 * PLANES, PAD, SIDE), F32), pltpu.VMEM((2 * SIDE, 2 * SIDE), F32)],
    )(listed, total_coef, coupling.reshape(2 * NPROJ, NPROJ), table, local)
    update = call(
        final_kernel,
        shape(2, PLANES, blocks, 8, SIDE),
        [vmem] * 2,
        [pltpu.VMEM((2, PLANES, blocks, 8, SIDE), F32), pltpu.SemaphoreType.DMA((2 * PLANES,))],
        outs=outside,
    )(
        total.reshape(2, PLANES, blocks, 8, SIDE), returned.reshape(2, blocks, PLANES, 8, SIDE)
    )
    return (update.reshape(wave.shape), density)


def solution(mesh):
    placed = (
        P(None, "orb", "grid", None, None),
        P("grid", None, None),
        P("orb"),
        P(),
        P(),
        P(),
        P(),
    )
    return jax.shard_map(
        whole_step,
        mesh=mesh,
        in_specs=placed,
        out_specs=(P(None, "orb", "grid", None, None), P("grid", "orb", None)),
        check_vma=False,
    )
```

```python
import math

import jax
import jax.numpy as jnp
import numpy as np
from jax import lax
from jax.experimental import pallas as pl
from jax.experimental.pallas import tpu as pltpu
from jax.sharding import PartitionSpec as P


spacing = 0.32
time_step = 0.1

SIDE = 128
BOX = 16
NPROJ = 8
PLANES = 4
PAD = SIDE + BOX
GROUP = 4
UNROLL = 8
FIELD = 136
COUNT = 5 * FIELD
F32 = jnp.float32
BF16 = jnp.bfloat16


def permuted(value, axis, target):
    count = lax.axis_size(axis)
    return lax.ppermute(value, axis, [(source, target(source) % count) for source in range(count)])


def kinetic_matrix(extent):
    counts = np.arange(extent)
    signed = np.where(counts < extent // 2, counts, counts - extent)
    waves = signed * (2.0 * math.pi / (extent * spacing))
    angles = (counts[:, None] * counts[None, :] % extent) * (2.0 * math.pi / extent)
    column = (np.cos(angles) * (0.5 * waves**2)[None, :]).sum(axis=1) / extent
    return column[(counts[:, None] - counts[None, :]) % extent]


def kinetic_halves(extent):
    matrix = kinetic_matrix(extent).astype(np.float32)
    high = matrix.astype(BF16)
    low = (matrix - high.astype(np.float32)).astype(BF16)
    row = np.concatenate([high, low], axis=1)
    return jnp.asarray(np.concatenate([row, row], axis=0))


def halves(value):
    high = value.astype(BF16)
    return high, (value - high.astype(F32)).astype(BF16)


def times_right(value, wide):
    product = jnp.dot(jnp.concatenate(halves(value), axis=1), wide, preferred_element_type=F32)
    return product[:, :SIDE] + product[:, SIDE:]


def times_left(pair, value):
    row = jnp.concatenate(halves(value), axis=1)
    product = jnp.dot(pair, jnp.concatenate([row, row], axis=0), preferred_element_type=F32)
    return product[:, :SIDE] + product[:, SIDE:]


def whole(memory=pltpu.VMEM):
    return pl.BlockSpec(memory_space=memory)


def call(kernel, out_shape, specs, scratch=(), outs=None, flops=1000000, moved=1000000):
    return pl.pallas_call(
        kernel,
        out_shape=out_shape,
        in_specs=specs,
        out_specs=jax.tree.map(lambda _: whole(), out_shape) if outs is None else outs,
        scratch_shapes=list(scratch),
        compiler_params=pltpu.CompilerParams(vmem_limit_bytes=12 * 1024 * 1024),
        cost_estimate=pl.CostEstimate(flops=flops, bytes_accessed=moved, transcendentals=0),
    )


def shape(*dims):
    return jax.ShapeDtypeStruct(dims, F32)


def density_kernel(occupation_ref, wave_ref, out_ref):
    occupation = occupation_ref[0]
    for plane in range(PLANES):
        real_part = wave_ref[0, plane]
        imag_part = wave_ref[1, plane]
        term = occupation * (real_part * real_part + imag_part * imag_part)
        for share in range(8):
            high, middle, low = share // 4, share // 2 % 2, share % 2
            out_ref[middle, high, low, plane] = term[share * 16 : share * 16 + 16]


def swap_blocks(tile, lane, row):
    for bit in (1, 2, 4):
        row_set = (row & bit) != 0
        lane_set = ((lane >> 4) & bit) != 0
        up = pltpu.roll(pltpu.roll(tile, 8 - bit, 0), 16 * bit, 1)
        down = pltpu.roll(pltpu.roll(tile, bit, 0), SIDE - 16 * bit, 1)
        tile = jnp.where(row_set == lane_set, tile, jnp.where(lane_set, up, down))
    return tile


def atom_place(first_plane, centres_ref, atom):
    depth = (first_plane - centres_ref[0, atom] + (BOX // 2 + SIDE)) & (SIDE - 1)
    start_y = (centres_ref[1, atom] + (SIDE - BOX // 2)) & (SIDE - 1)
    start_z = (centres_ref[2, atom] + (SIDE - BOX // 2)) & (SIDE - 1)
    return depth, start_y, start_z


def table_row(depth, plane, kind):
    slot = (depth + plane) & (SIDE - 1)
    return jnp.where(slot < BOX, kind * BOX + slot, 2 * BOX)


def entry(listed_ref, index):
    return [listed_ref[field * FIELD + index] for field in range(5)]


def group_count(listed_ref):
    return (listed_ref[COUNT] + (GROUP - 1)) // GROUP


def project_kernel(listed_ref, wave_ref, projectors_ref, coef_ref, table_ref, padded, sums):
    lane = lax.broadcasted_iota(jnp.int32, (8, SIDE), 1)
    row = lax.broadcasted_iota(jnp.int32, (8, SIDE), 0)

    def widen(index, carry):
        padded[index, 0:SIDE, :] = wave_ref[index]
        padded[index, SIDE:PAD, :] = wave_ref[index, 0:BOX, :]
        return carry

    lax.fori_loop(0, 2 * PLANES, widen, 0)
    sums[...] = jnp.zeros_like(sums)

    def fill(index, carry):
        for half in range(2):
            tile = projectors_ref[index, :, half * SIDE : (half + 1) * SIDE]
            table_ref[index, half * 8 : half * 8 + 8, :] = swap_blocks(tile, lane, row)
        return carry

    lax.fori_loop(0, 2 * BOX, fill, 0, unroll=UNROLL)
    table_ref[2 * BOX] = jnp.zeros((BOX, SIDE), F32)
    inner = lane & (BOX - 1)

    def group_step(step, carry):
        for offset in range(GROUP):
            listed, depth, start_y, start_z, kind = entry(listed_ref, step * GROUP + offset)
            picks = (inner + start_z) & (SIDE - 1)
            totals = [jnp.zeros((8, SIDE), F32), jnp.zeros((8, SIDE), F32)]
            for plane in range(PLANES):
                index = table_row(depth, plane, kind)
                for half in range(2):
                    weights = table_ref[index, half * 8 : half * 8 + 8, :]
                    for part in range(2):
                        values = padded[part * PLANES + plane, pl.ds(start_y + half * 8, 8), :]
                        values = jnp.take_along_axis(values, picks, axis=1)
                        totals[part] = totals[part] + values * weights
            for part in range(2):
                sums[part, pl.ds(listed, 1), :] = jnp.sum(totals[part], axis=0, keepdims=True)
        return carry

    lax.fori_loop(0, group_count(listed_ref), group_step, 0)
    groups = ((lax.broadcasted_iota(jnp.int32, (NPROJ, 2 * SIDE), 1) >> 4) & (NPROJ - 1)) == (
        lax.broadcasted_iota(jnp.int32, (NPROJ, 2 * SIDE), 0)
    )
    rows = jnp.concatenate([sums[part, 0:SIDE, :] for part in range(2)], axis=0)
    coef = lax.dot_general(
        groups.astype(F32).astype(BF16),
        jnp.concatenate(halves(rows), axis=1),
        (((1,), (1,)), ((), ())),
        preferred_element_type=F32,
    )
    coef_ref[0:8, :] = coef[:, :SIDE]
    coef_ref[8:16, :] = coef[:, SIDE:]


def spread_kernel(
    listed_ref,
    coef_ref,
    coupling_ref,
    table_ref,
    local_ref,
    out_ref,
    padded,
    scaled,
):
    lane = lax.broadcasted_iota(jnp.int32, (8, SIDE), 1)
    groups = (lax.broadcasted_iota(jnp.int32, (2 * NPROJ, 2 * SIDE), 1) >> 4) == (
        lax.broadcasted_iota(jnp.int32, (2 * NPROJ, 2 * SIDE), 0)
    )
    groups = groups.astype(F32).astype(BF16)
    first, second = (half.astype(F32) for half in halves(coupling_ref[...]))
    mixing = lax.dot_general(
        jnp.concatenate([first, second], axis=1).astype(BF16),
        groups,
        (((0,), (0,)), ((), ())),
        preferred_element_type=F32,
    )
    both = jnp.concatenate([coef_ref[0:8, :], coef_ref[8:16, :]], axis=1)
    first, second = (half.astype(F32) for half in halves(both))
    scaled[...] = lax.dot_general(
        jnp.concatenate([first, first, second], axis=0).astype(BF16),
        jnp.concatenate([mixing[0:8], mixing[8:16], mixing[0:8]], axis=0).astype(BF16),
        (((0,), (0,)), ((), ())),
        preferred_element_type=F32,
    )

    def widen(index, carry):
        padded[index, 0:SIDE, :] = local_ref[index]
        padded[index, SIDE:PAD, :] = jnp.zeros((BOX, SIDE), F32)
        return carry

    lax.fori_loop(0, 2 * PLANES, widen, 0)

    def group_step(step, carry):
        for offset in range(GROUP):
            listed, depth, start_y, start_z, kind = entry(listed_ref, step * GROUP + offset)
            atom = jnp.minimum(listed, SIDE - 1)
            inside = ((lane - start_z) & (SIDE - 1)) < BOX
            both = [scaled[pl.ds(part * SIDE + atom, 1), :] for part in range(2)]
            factors = [jnp.where(kind == 0, pair[:, :SIDE], pair[:, SIDE:]) for pair in both]
            added = []
            for plane in range(PLANES):
                index = table_row(depth, plane, kind)
                for half in range(2):
                    weights = table_ref[index, half * 8 : half * 8 + 8, :]
                    for part in range(2):
                        values = weights * factors[part]
                        values = values + pltpu.roll(values, 64, 1)
                        values = values + pltpu.roll(values, 32, 1)
                        values = values + pltpu.roll(values, 16, 1)
                        values = jnp.where(inside, pltpu.roll(values, start_z, 1), 0.0)
                        added.append((part * PLANES + plane, start_y + half * 8, values))
            for where, start, values in added:
                padded[where, pl.ds(start, 8), :] = padded[where, pl.ds(start, 8), :] + values
        return carry

    lax.fori_loop(0, group_count(listed_ref), group_step, 0)

    def narrow(index, carry):
        out_ref[index, 0:BOX, :] = padded[index, 0:BOX, :] + padded[index, SIDE:PAD, :]
        out_ref[index, BOX:SIDE, :] = padded[index, BOX:SIDE, :]
        return carry

    lax.fori_loop(0, 2 * PLANES, narrow, 0)


def local_kernel(wave_ref, potential_ref, wide_ref, out_ref):
    wide = wide_ref[...]
    pair = wide_ref[0:SIDE, :]
    for index in range(2 * PLANES):
        value = wave_ref[index]
        out_ref[index] = times_right(value, wide) + times_left(pair, value) + potential_ref[index % PLANES] * value


def depth_kernel(value_ref, wide_ref, out_ref, rows, sems):
    pair = wide_ref[0:SIDE, :]
    copies = []
    for row in range(8):
        rows[row] = times_left(pair, value_ref[pl.ds(row, SIDE, stride=8), :])
        copies.append(pltpu.make_async_copy(rows.at[row], out_ref.at[:, row, :], sems.at[row]))
        copies[-1].start()
    for copy in copies:
        copy.wait()


def list_part(first_plane, centres_ref, listed_ref, start, stop, count):
    top = first_plane + (BOX // 2 + SIDE + PLANES - 1)

    def list_step(atom, count):
        reach = (top - centres_ref[0, atom]) & (SIDE - 1)
        listed_ref[count] = atom
        return count + jnp.where(reach < BOX + PLANES - 1, 1, 0)

    return lax.fori_loop(start, stop, list_step, count, unroll=8)


def list_details(first_plane, centres_ref, species_ref, listed_ref, count):
    listed_ref[COUNT] = count

    def detail_step(index, carry):
        atom = listed_ref[index]
        place = atom_place(first_plane, centres_ref, atom)
        for field, value in enumerate((*place, species_ref[atom])):
            listed_ref[(field + 1) * FIELD + index] = value
        return carry

    lax.fori_loop(0, count, detail_step, 0)
    for extra in range(GROUP):
        for field, value in enumerate((SIDE, SIDE // 2, 0, 0, 0)):
            listed_ref[field * FIELD + count + extra] = jnp.int32(value)


def pack_kernel(
    first_ref,
    wave_ref,
    centres_ref,
    species_ref,
    out_ref,
    listed_out_ref,
    held,
    centres,
    species,
    listed,
    in_sems,
    out_sems,
    list_sems,
):
    places = [(part, plane) for part in range(2) for plane in range(PLANES)]
    arriving = [
        pltpu.make_async_copy(wave_ref.at[place], held.at[place], in_sems.at[slot]) for slot, place in enumerate(places)
    ]
    leaving = [
        pltpu.make_async_copy(held.at[part, plane], out_ref.at[part, :, plane], out_sems.at[slot])
        for slot, (part, plane) in enumerate(places)
    ]
    tables = [
        pltpu.make_async_copy(centres_ref, centres, list_sems.at[0]),
        pltpu.make_async_copy(species_ref, species, list_sems.at[1]),
    ]
    listing = pltpu.make_async_copy(listed, listed_out_ref, list_sems.at[2])
    for copy in tables + arriving:
        copy.start()
    for copy in tables:
        copy.wait()
    count = jnp.int32(0)
    for slot in range(2 * PLANES):
        if slot % 2 == 0:
            share = SIDE // PLANES
            count = list_part(first_ref[0], centres, listed, slot // 2 * share, (slot // 2 + 1) * share, count)
        arriving[slot].wait()
        leaving[slot].start()
    list_details(first_ref[0], centres, species, listed, count)
    listing.start()
    for copy in leaving:
        copy.wait()
    listing.wait()


def final_kernel(local_ref, depth_ref, mine_ref, first_ref, second_ref, third_ref, out_ref, density_ref, held, sums, sems):
    half_step = 0.5 * time_step
    sums[...] = (mine_ref[...] + first_ref[...]) + (second_ref[...] + third_ref[...])
    copies = [pltpu.make_async_copy(sums, density_ref, sems.at[2 * PLANES])]
    copies[-1].start()
    for plane in range(PLANES):
        for part, sign in ((0, half_step), (1, -half_step)):
            held[part, plane] = sign * (local_ref[1 - part, plane] + depth_ref[1 - part, :, plane])
            copies.append(
                pltpu.make_async_copy(held.at[part, plane], out_ref.at[part, plane], sems.at[part * PLANES + plane])
            )
            copies[-1].start()
    for copy in copies:
        copy.wait()


def whole_step(wave, potential, occupations, centres, species, projectors, coupling):
    vmem, smem, outside = whole(), whole(pltpu.SMEM), whole(pl.ANY)
    wide = kinetic_halves(SIDE)
    blocks = SIDE // 8
    first_plane = jnp.reshape(lax.axis_index("grid") * PLANES, (1,)).astype(jnp.int32)
    tiles = wave.reshape(2, PLANES, blocks, 8, SIDE)
    planes = wave.reshape(2 * PLANES, SIDE, SIDE)
    table_in = projectors.reshape(2 * BOX, NPROJ, BOX * BOX)

    sent, listed = call(
        pack_kernel,
        (shape(2, blocks, PLANES, 8, SIDE), jax.ShapeDtypeStruct((COUNT + FIELD,), jnp.int32)),
        [smem] + [whole(pltpu.HBM)] * 3,
        [
            pltpu.VMEM((2, PLANES, blocks, 8, SIDE), F32),
            pltpu.SMEM((3, SIDE), jnp.int32),
            pltpu.SMEM((SIDE,), jnp.int32),
            pltpu.SMEM((COUNT + FIELD,), jnp.int32),
            pltpu.SemaphoreType.DMA((2 * PLANES,)),
            pltpu.SemaphoreType.DMA((2 * PLANES,)),
            pltpu.SemaphoreType.DMA((3,)),
        ],
        outs=(outside, outside),
    )(first_plane, *(pltpu.with_memory_space_constraint(value, pltpu.HBM) for value in (tiles, centres, species)))
    sent = sent.reshape(2 * blocks, PLANES, 8, SIDE)
    columns = lax.all_to_all(sent, "grid", 0, 0, tiled=True)

    terms = call(density_kernel, shape(2, 2, 2, PLANES, 16, SIDE), [smem, vmem])(
        occupations, wave.reshape(2, PLANES, SIDE, SIDE)
    )
    coef, table = call(
        project_kernel,
        (shape(2 * NPROJ, SIDE), shape(2 * BOX + 1, BOX, SIDE)),
        [smem, vmem, vmem],
        [pltpu.VMEM((2 * PLANES, PAD, SIDE), F32), pltpu.VMEM((2, SIDE + 8, SIDE), F32)],
    )(listed, planes, table_in)
    coef = coef + permuted(coef, "grid", lambda place: place ^ 1)
    coef = coef + permuted(coef, "grid", lambda place: place ^ 2)
    above = permuted(coef, "grid", lambda place: place + 4)
    below = permuted(coef, "grid", lambda place: place - 4)
    total_coef = coef + above + below

    local = call(local_kernel, shape(2 * PLANES, SIDE, SIDE), [vmem] * 3)(planes, potential, wide)

    place = lax.axis_index("orb")
    middle, high_bit, low_bit = place // 2 % 2, place // 4, place % 2
    kept = lax.dynamic_index_in_dim(terms, middle, 0, keepdims=False)
    given = lax.dynamic_index_in_dim(terms, 1 - middle, 0, keepdims=False)
    terms = kept + permuted(given, "orb", lambda source: source ^ 2)

    def share_of(high, low):
        return lax.dynamic_slice(terms, (high, low, 0, 0, 0), (1, 1, PLANES, 16, SIDE))[0, 0]

    shares = [
        share_of(high_bit, low_bit),
        permuted(share_of(1 - high_bit, low_bit), "orb", lambda source: source ^ 4),
        permuted(share_of(high_bit, 1 - low_bit), "orb", lambda source: source ^ 1),
        permuted(share_of(1 - high_bit, 1 - low_bit), "orb", lambda source: source ^ 5),
    ]

    depth = call(
        depth_kernel,
        shape(SIDE, 8, SIDE),
        [vmem] * 2,
        [pltpu.VMEM((8, SIDE, SIDE), F32), pltpu.SemaphoreType.DMA((8,))],
        outs=outside,
    )(columns.reshape(8 * SIDE, SIDE), wide)
    returned = lax.all_to_all(depth.reshape(2 * blocks, PLANES, 8, SIDE), "grid", 0, 0, tiled=True)

    total = call(
        spread_kernel,
        shape(2 * PLANES, SIDE, SIDE),
        [smem, vmem, vmem, vmem, vmem],
        [pltpu.VMEM((2 * PLANES, PAD, SIDE), F32), pltpu.VMEM((2 * SIDE, 2 * SIDE), F32)],
    )(listed, total_coef, coupling.reshape(2 * NPROJ, NPROJ), table, local)
    update, density = call(
        final_kernel,
        (shape(2, PLANES, blocks, 8, SIDE), shape(PLANES, 16, SIDE)),
        [vmem] * 6,
        [
            pltpu.VMEM((2, PLANES, blocks, 8, SIDE), F32),
            pltpu.VMEM((PLANES, 16, SIDE), F32),
            pltpu.SemaphoreType.DMA((2 * PLANES + 1,)),
        ],
        outs=(outside, outside),
    )(
        total.reshape(2, PLANES, blocks, 8, SIDE),
        returned.reshape(2, blocks, PLANES, 8, SIDE),
        *shares,
    )
    return (update.reshape(wave.shape), density)


def solution(mesh):
    placed = (
        P(None, "orb", "grid", None, None),
        P("grid", None, None),
        P("orb"),
        P(),
        P(),
        P(),
        P(),
    )
    return jax.shard_map(
        whole_step,
        mesh=mesh,
        in_specs=placed,
        out_specs=(P(None, "orb", "grid", None, None), P("grid", "orb", None)),
        check_vma=False,
    )
```

```python
import math

import jax
import jax.numpy as jnp
import numpy as np
from jax import lax
from jax.experimental import pallas as pl
from jax.experimental.pallas import tpu as pltpu
from jax.sharding import PartitionSpec as P


spacing = 0.32
time_step = 0.1

SIDE = 128
BOX = 16
NPROJ = 8
PLANES = 4
PAD = SIDE + BOX
GROUP = 4
UNROLL = 8
FIELD = 136
COUNT = 5 * FIELD
F32 = jnp.float32
BF16 = jnp.bfloat16


def permuted(value, axis, target):
    count = lax.axis_size(axis)
    return lax.ppermute(value, axis, [(source, target(source) % count) for source in range(count)])


def kinetic_matrix(extent):
    counts = np.arange(extent)
    signed = np.where(counts < extent // 2, counts, counts - extent)
    waves = signed * (2.0 * math.pi / (extent * spacing))
    angles = (counts[:, None] * counts[None, :] % extent) * (2.0 * math.pi / extent)
    column = (np.cos(angles) * (0.5 * waves**2)[None, :]).sum(axis=1) / extent
    return column[(counts[:, None] - counts[None, :]) % extent]


def kinetic_halves(extent):
    matrix = kinetic_matrix(extent).astype(np.float32)
    high = matrix.astype(BF16)
    low = (matrix - high.astype(np.float32)).astype(BF16)
    row = np.concatenate([high, low], axis=1)
    return jnp.asarray(np.concatenate([row, row], axis=0))


def halves(value):
    high = value.astype(BF16)
    return high, (value - high.astype(F32)).astype(BF16)


def times_right(value, wide):
    product = jnp.dot(jnp.concatenate(halves(value), axis=1), wide, preferred_element_type=F32)
    return product[:, :SIDE] + product[:, SIDE:]


def times_left(pair, value):
    row = jnp.concatenate(halves(value), axis=1)
    product = jnp.dot(pair, jnp.concatenate([row, row], axis=0), preferred_element_type=F32)
    return product[:, :SIDE] + product[:, SIDE:]


def whole(memory=pltpu.VMEM):
    return pl.BlockSpec(memory_space=memory)


def call(kernel, out_shape, specs, scratch=(), outs=None, flops=1000000, moved=1000000):
    return pl.pallas_call(
        kernel,
        out_shape=out_shape,
        in_specs=specs,
        out_specs=jax.tree.map(lambda _: whole(), out_shape) if outs is None else outs,
        scratch_shapes=list(scratch),
        compiler_params=pltpu.CompilerParams(vmem_limit_bytes=12 * 1024 * 1024),
        cost_estimate=pl.CostEstimate(flops=flops, bytes_accessed=moved, transcendentals=0),
    )


def shape(*dims):
    return jax.ShapeDtypeStruct(dims, F32)


def density_kernel(occupation_ref, wave_ref, out_ref):
    occupation = occupation_ref[0]
    for plane in range(PLANES):
        real_part = wave_ref[0, plane]
        imag_part = wave_ref[1, plane]
        term = occupation * (real_part * real_part + imag_part * imag_part)
        for share in range(8):
            high, middle, low = share // 4, share // 2 % 2, share % 2
            out_ref[middle, high, low, plane] = term[share * 16 : share * 16 + 16]


def swap_blocks(tile, lane, row):
    for bit in (1, 2, 4):
        row_set = (row & bit) != 0
        lane_set = ((lane >> 4) & bit) != 0
        up = pltpu.roll(pltpu.roll(tile, 8 - bit, 0), 16 * bit, 1)
        down = pltpu.roll(pltpu.roll(tile, bit, 0), SIDE - 16 * bit, 1)
        tile = jnp.where(row_set == lane_set, tile, jnp.where(lane_set, up, down))
    return tile


def atom_place(first_plane, centres_ref, atom):
    depth = (first_plane - centres_ref[0, atom] + (BOX // 2 + SIDE)) & (SIDE - 1)
    start_y = (centres_ref[1, atom] + (SIDE - BOX // 2)) & (SIDE - 1)
    start_z = (centres_ref[2, atom] + (SIDE - BOX // 2)) & (SIDE - 1)
    return depth, start_y, start_z


def table_row(depth, plane, kind):
    slot = (depth + plane) & (SIDE - 1)
    return jnp.where(slot < BOX, kind * BOX + slot, 2 * BOX)


def entry(listed_ref, index):
    return [listed_ref[field * FIELD + index] for field in range(5)]


def group_count(listed_ref):
    return (listed_ref[COUNT] + (GROUP - 1)) // GROUP


def project_kernel(
    first_ref,
    centres_ref,
    species_ref,
    wave_ref,
    projectors_ref,
    coef_ref,
    table_ref,
    listed_ref,
    padded,
    sums,
    centres,
    species,
    sems,
):
    arriving = [
        pltpu.make_async_copy(centres_ref, centres, sems.at[0]),
        pltpu.make_async_copy(species_ref, species, sems.at[1]),
    ]
    for copy in arriving:
        copy.start()
    lane = lax.broadcasted_iota(jnp.int32, (8, SIDE), 1)
    row = lax.broadcasted_iota(jnp.int32, (8, SIDE), 0)

    def widen(index, carry):
        padded[index, 0:SIDE, :] = wave_ref[index]
        padded[index, SIDE:PAD, :] = wave_ref[index, 0:BOX, :]
        return carry

    lax.fori_loop(0, 2 * PLANES, widen, 0)
    sums[...] = jnp.zeros_like(sums)

    def fill(index, carry):
        for half in range(2):
            tile = projectors_ref[index, :, half * SIDE : (half + 1) * SIDE]
            table_ref[index, half * 8 : half * 8 + 8, :] = swap_blocks(tile, lane, row)
        return carry

    lax.fori_loop(0, 2 * BOX, fill, 0, unroll=UNROLL)
    table_ref[2 * BOX] = jnp.zeros((BOX, SIDE), F32)
    for copy in arriving:
        copy.wait()
    count = list_part(first_ref[0], centres, listed_ref, 0, SIDE, jnp.int32(0))
    list_details(first_ref[0], centres, species, listed_ref, count)
    inner = lane & (BOX - 1)

    def group_step(step, carry):
        for offset in range(GROUP):
            listed, depth, start_y, start_z, kind = entry(listed_ref, step * GROUP + offset)
            picks = (inner + start_z) & (SIDE - 1)
            totals = [jnp.zeros((8, SIDE), F32), jnp.zeros((8, SIDE), F32)]
            for plane in range(PLANES):
                index = table_row(depth, plane, kind)
                for half in range(2):
                    weights = table_ref[index, half * 8 : half * 8 + 8, :]
                    for part in range(2):
                        values = padded[part * PLANES + plane, pl.ds(start_y + half * 8, 8), :]
                        values = jnp.take_along_axis(values, picks, axis=1)
                        totals[part] = totals[part] + values * weights
            for part in range(2):
                sums[part, pl.ds(listed, 1), :] = jnp.sum(totals[part], axis=0, keepdims=True)
        return carry

    lax.fori_loop(0, group_count(listed_ref), group_step, 0)
    groups = ((lax.broadcasted_iota(jnp.int32, (NPROJ, 2 * SIDE), 1) >> 4) & (NPROJ - 1)) == (
        lax.broadcasted_iota(jnp.int32, (NPROJ, 2 * SIDE), 0)
    )
    rows = jnp.concatenate([sums[part, 0:SIDE, :] for part in range(2)], axis=0)
    coef = lax.dot_general(
        groups.astype(F32).astype(BF16),
        jnp.concatenate(halves(rows), axis=1),
        (((1,), (1,)), ((), ())),
        preferred_element_type=F32,
    )
    coef_ref[0:8, :] = coef[:, :SIDE]
    coef_ref[8:16, :] = coef[:, SIDE:]


def spread_kernel(
    listed_ref,
    coef_ref,
    coupling_ref,
    table_ref,
    local_ref,
    out_ref,
    padded,
    scaled,
):
    lane = lax.broadcasted_iota(jnp.int32, (8, SIDE), 1)
    groups = (lax.broadcasted_iota(jnp.int32, (2 * NPROJ, 2 * SIDE), 1) >> 4) == (
        lax.broadcasted_iota(jnp.int32, (2 * NPROJ, 2 * SIDE), 0)
    )
    groups = groups.astype(F32).astype(BF16)
    first, second = (half.astype(F32) for half in halves(coupling_ref[...]))
    mixing = lax.dot_general(
        jnp.concatenate([first, second], axis=1).astype(BF16),
        groups,
        (((0,), (0,)), ((), ())),
        preferred_element_type=F32,
    )
    both = jnp.concatenate([coef_ref[0:8, :], coef_ref[8:16, :]], axis=1)
    first, second = (half.astype(F32) for half in halves(both))
    scaled[...] = lax.dot_general(
        jnp.concatenate([first, first, second], axis=0).astype(BF16),
        jnp.concatenate([mixing[0:8], mixing[8:16], mixing[0:8]], axis=0).astype(BF16),
        (((0,), (0,)), ((), ())),
        preferred_element_type=F32,
    )

    def widen(index, carry):
        padded[index, 0:SIDE, :] = local_ref[index]
        padded[index, SIDE:PAD, :] = jnp.zeros((BOX, SIDE), F32)
        return carry

    lax.fori_loop(0, 2 * PLANES, widen, 0)

    def group_step(step, carry):
        for offset in range(GROUP):
            listed, depth, start_y, start_z, kind = entry(listed_ref, step * GROUP + offset)
            atom = jnp.minimum(listed, SIDE - 1)
            inside = ((lane - start_z) & (SIDE - 1)) < BOX
            both = [scaled[pl.ds(part * SIDE + atom, 1), :] for part in range(2)]
            factors = [jnp.where(kind == 0, pair[:, :SIDE], pair[:, SIDE:]) for pair in both]
            added = []
            for plane in range(PLANES):
                index = table_row(depth, plane, kind)
                for half in range(2):
                    weights = table_ref[index, half * 8 : half * 8 + 8, :]
                    for part in range(2):
                        values = weights * factors[part]
                        values = values + pltpu.roll(values, 64, 1)
                        values = values + pltpu.roll(values, 32, 1)
                        values = values + pltpu.roll(values, 16, 1)
                        values = jnp.where(inside, pltpu.roll(values, start_z, 1), 0.0)
                        added.append((part * PLANES + plane, start_y + half * 8, values))
            for where, start, values in added:
                padded[where, pl.ds(start, 8), :] = padded[where, pl.ds(start, 8), :] + values
        return carry

    lax.fori_loop(0, group_count(listed_ref), group_step, 0)

    def narrow(index, carry):
        out_ref[index, 0:BOX, :] = padded[index, 0:BOX, :] + padded[index, SIDE:PAD, :]
        out_ref[index, BOX:SIDE, :] = padded[index, BOX:SIDE, :]
        return carry

    lax.fori_loop(0, 2 * PLANES, narrow, 0)


def local_kernel(wave_ref, potential_ref, wide_ref, out_ref):
    wide = wide_ref[...]
    pair = wide_ref[0:SIDE, :]
    for index in range(2 * PLANES):
        value = wave_ref[index]
        out_ref[index] = times_right(value, wide) + times_left(pair, value) + potential_ref[index % PLANES] * value


def depth_kernel(value_ref, wide_ref, out_ref, rows, sems):
    pair = wide_ref[0:SIDE, :]
    copies = []
    for row in range(8):
        rows[row] = times_left(pair, value_ref[pl.ds(row, SIDE, stride=8), :])
        copies.append(pltpu.make_async_copy(rows.at[row], out_ref.at[:, row, :], sems.at[row]))
        copies[-1].start()
    for copy in copies:
        copy.wait()


def list_part(first_plane, centres_ref, listed_ref, start, stop, count):
    top = first_plane + (BOX // 2 + SIDE + PLANES - 1)

    def list_step(atom, count):
        reach = (top - centres_ref[0, atom]) & (SIDE - 1)
        listed_ref[count] = atom
        return count + jnp.where(reach < BOX + PLANES - 1, 1, 0)

    return lax.fori_loop(start, stop, list_step, count, unroll=8)


def list_details(first_plane, centres_ref, species_ref, listed_ref, count):
    listed_ref[COUNT] = count

    def detail_step(index, carry):
        atom = listed_ref[index]
        place = atom_place(first_plane, centres_ref, atom)
        for field, value in enumerate((*place, species_ref[atom])):
            listed_ref[(field + 1) * FIELD + index] = value
        return carry

    lax.fori_loop(0, count, detail_step, 0)
    for extra in range(GROUP):
        for field, value in enumerate((SIDE, SIDE // 2, 0, 0, 0)):
            listed_ref[field * FIELD + count + extra] = jnp.int32(value)


def pack_kernel(wave_ref, out_ref, held, in_sems, out_sems):
    places = [(part, plane) for part in range(2) for plane in range(PLANES)]
    arriving = [
        pltpu.make_async_copy(wave_ref.at[place], held.at[place], in_sems.at[slot]) for slot, place in enumerate(places)
    ]
    leaving = [
        pltpu.make_async_copy(held.at[part, plane], out_ref.at[part, :, plane], out_sems.at[slot])
        for slot, (part, plane) in enumerate(places)
    ]
    for copy in arriving:
        copy.start()
    for first, second in zip(arriving, leaving):
        first.wait()
        second.start()
    for copy in leaving:
        copy.wait()


def final_kernel(local_ref, depth_ref, mine_ref, first_ref, second_ref, third_ref, out_ref, density_ref, held, sums, sems):
    half_step = 0.5 * time_step
    sums[...] = (mine_ref[...] + first_ref[...]) + (second_ref[...] + third_ref[...])
    copies = [pltpu.make_async_copy(sums, density_ref, sems.at[2 * PLANES])]
    copies[-1].start()
    for plane in range(PLANES):
        for part, sign in ((0, half_step), (1, -half_step)):
            held[part, plane] = sign * (local_ref[1 - part, plane] + depth_ref[1 - part, :, plane])
            copies.append(
                pltpu.make_async_copy(held.at[part, plane], out_ref.at[part, plane], sems.at[part * PLANES + plane])
            )
            copies[-1].start()
    for copy in copies:
        copy.wait()


def in_place(value):
    return pltpu.with_memory_space_constraint(value, pltpu.HBM)


def whole_step(wave, potential, occupations, centres, species, projectors, coupling):
    vmem, smem, outside = whole(), whole(pltpu.SMEM), whole(pl.ANY)
    wide = kinetic_halves(SIDE)
    blocks = SIDE // 8
    first_plane = jnp.reshape(lax.axis_index("grid") * PLANES, (1,)).astype(jnp.int32)
    tiles = wave.reshape(2, PLANES, blocks, 8, SIDE)
    planes = wave.reshape(2 * PLANES, SIDE, SIDE)
    table_in = projectors.reshape(2 * BOX, NPROJ, BOX * BOX)

    sent = call(
        pack_kernel,
        shape(2, blocks, PLANES, 8, SIDE),
        [whole(pltpu.HBM)],
        [
            pltpu.VMEM((2, PLANES, blocks, 8, SIDE), F32),
            pltpu.SemaphoreType.DMA((2 * PLANES,)),
            pltpu.SemaphoreType.DMA((2 * PLANES,)),
        ],
        outs=outside,
    )(in_place(tiles)).reshape(2 * blocks, PLANES, 8, SIDE)
    columns = lax.all_to_all(sent, "grid", 0, 0, tiled=True)

    terms = call(density_kernel, shape(2, 2, 2, PLANES, 16, SIDE), [smem, vmem])(
        occupations, wave.reshape(2, PLANES, SIDE, SIDE)
    )
    coef, table, listed = call(
        project_kernel,
        (
            shape(2 * NPROJ, SIDE),
            shape(2 * BOX + 1, BOX, SIDE),
            jax.ShapeDtypeStruct((COUNT + FIELD,), jnp.int32),
        ),
        [smem, whole(pltpu.HBM), whole(pltpu.HBM), vmem, vmem],
        [
            pltpu.VMEM((2 * PLANES, PAD, SIDE), F32),
            pltpu.VMEM((2, SIDE + 8, SIDE), F32),
            pltpu.SMEM((3, SIDE), jnp.int32),
            pltpu.SMEM((SIDE,), jnp.int32),
            pltpu.SemaphoreType.DMA((2,)),
        ],
        outs=(vmem, vmem, smem),
    )(first_plane, in_place(centres), in_place(species), planes, table_in)
    coef = coef + permuted(coef, "grid", lambda place: place ^ 1)
    coef = coef + permuted(coef, "grid", lambda place: place ^ 2)
    above = permuted(coef, "grid", lambda place: place + 4)
    below = permuted(coef, "grid", lambda place: place - 4)
    total_coef = coef + above + below

    local = call(local_kernel, shape(2 * PLANES, SIDE, SIDE), [vmem] * 3)(planes, potential, wide)

    place = lax.axis_index("orb")
    middle, high_bit, low_bit = place // 2 % 2, place // 4, place % 2
    kept = lax.dynamic_index_in_dim(terms, middle, 0, keepdims=False)
    given = lax.dynamic_index_in_dim(terms, 1 - middle, 0, keepdims=False)
    terms = kept + permuted(given, "orb", lambda source: source ^ 2)

    def share_of(high, low):
        return lax.dynamic_slice(terms, (high, low, 0, 0, 0), (1, 1, PLANES, 16, SIDE))[0, 0]

    shares = [
        share_of(high_bit, low_bit),
        permuted(share_of(1 - high_bit, low_bit), "orb", lambda source: source ^ 4),
        permuted(share_of(high_bit, 1 - low_bit), "orb", lambda source: source ^ 1),
        permuted(share_of(1 - high_bit, 1 - low_bit), "orb", lambda source: source ^ 5),
    ]

    depth = call(
        depth_kernel,
        shape(SIDE, 8, SIDE),
        [vmem] * 2,
        [pltpu.VMEM((8, SIDE, SIDE), F32), pltpu.SemaphoreType.DMA((8,))],
        outs=outside,
    )(columns.reshape(8 * SIDE, SIDE), wide)
    returned = lax.all_to_all(depth.reshape(2 * blocks, PLANES, 8, SIDE), "grid", 0, 0, tiled=True)

    total = call(
        spread_kernel,
        shape(2 * PLANES, SIDE, SIDE),
        [smem, vmem, vmem, vmem, vmem],
        [pltpu.VMEM((2 * PLANES, PAD, SIDE), F32), pltpu.VMEM((2 * SIDE, 2 * SIDE), F32)],
    )(listed, total_coef, coupling.reshape(2 * NPROJ, NPROJ), table, local)
    update, density = call(
        final_kernel,
        (shape(2, PLANES, blocks, 8, SIDE), shape(PLANES, 16, SIDE)),
        [vmem] * 6,
        [
            pltpu.VMEM((2, PLANES, blocks, 8, SIDE), F32),
            pltpu.VMEM((PLANES, 16, SIDE), F32),
            pltpu.SemaphoreType.DMA((2 * PLANES + 1,)),
        ],
        outs=(outside, outside),
    )(
        total.reshape(2, PLANES, blocks, 8, SIDE),
        returned.reshape(2, blocks, PLANES, 8, SIDE),
        *shares,
    )
    return (update.reshape(wave.shape), density)


def solution(mesh):
    placed = (
        P(None, "orb", "grid", None, None),
        P("grid", None, None),
        P("orb"),
        P(),
        P(),
        P(),
        P(),
    )
    return jax.shard_map(
        whole_step,
        mesh=mesh,
        in_specs=placed,
        out_specs=(P(None, "orb", "grid", None, None), P("grid", "orb", None)),
        check_vma=False,
    )
```
